128 devices in a mesh: row: 8 (over x_lo, z), col: 16 (over x_hi, y, core).
Axes of the slice: x: 4 (x_hi: 2, x_lo: 2; x = x_hi * 2 + x_lo), y: 4, z: 4, core: 2. Of those that a mesh axis runs over, the one named last changes fastest.
Arguments:
- child_rhs: bfloat16 [2, 16384, 256], P(None, 'row', 'col'), may hold values from -6 to 6
- child_inverse_t: bfloat16 [2, 16384, 8192], P(None, 'row', 'col'), may hold values from -0.046875 to 0.046875
- boundary_tiles: bfloat16 [2, 16384, 8192], P(None, 'row', 'col'), may hold values from -0.046875 to 0.046875
- boundary_lists: int32 [2, 64], replicated, may hold values from 0 to 95, as said below
- root_rhs: bfloat16 [2, 12288, 256], P(None, 'col'), may hold values from -6 to 6
- root_inverse: bfloat16 [2, 12288, 12288], P(None, 'row', 'col'), may hold values from -0.0390625 to 0.0390625
Outputs:
- child_solution: bfloat16 [2, 8192, 512], P(None, 'col', 'row')
- root_solution: float32 [2, 12288, 256], P(None, 'row', 'col')
The draws below stay inside these ranges and needn't reach their ends.
Inputs may be any that keep to these rules, and one draw needn't show every extreme that they name: `boundary_lists`: within one child the 64 entries name distinct root blocks; the two children together name every one of the 96 root blocks.
All inputs are finite; a program needn't handle non-finite values.
Results may differ from the reference program's by a relative error of at most 0.0055.
Values may be sent and summed in bfloat16 or wider, within the bound.
A program may use at most 128 MiB of HBM per device.

```python
import jax
import jax.numpy as jnp
from jax import lax

P_SIZE = 8192
CB = 8192
R = 12288
NRHS = 256
BLK = 128
NBLK = 64
RB = 96


def draw_boundary_lists(key, part):
    order = jax.random.permutation(key, RB).astype(jnp.int32)
    first_child = order[:NBLK]
    second_child = jax.random.permutation(jax.random.fold_in(key, 7), order[RB - NBLK:]).astype(jnp.int32)
    return jnp.stack((first_child, second_child)).astype(jnp.int32)


def level_of(rng, dims, split, smallest, largest):
    def one(axis_at, blocks):
        steps = jax.random.uniform(jax.random.fold_in(jax.random.fold_in(rng, 6), axis_at), (blocks,), jnp.float32, smallest / len(split), largest / len(split))
        return jnp.repeat(jnp.exp(steps), dims[axis_at] // blocks).reshape((-1,) + (1,) * (len(dims) - axis_at - 1))

    gain = one(*split[0])
    for cut in split[1:]:
        gain = gain * one(*cut)
    return gain


def gaussian(own_key, dims, width, limit, split=(), held_as=jnp.bfloat16):
    entries = jax.random.normal(own_key, dims, jnp.float32) * width
    if len(split) > 0:
        entries = level_of(own_key, dims, split, -0.22, 0.18) * entries
    return jnp.clip(entries, min=-limit, max=limit).astype(held_as)


def setup_inputs(seed: int = 0) -> dict:
    streams_of = jax.random.split(jax.random.key(seed), 7)
    return {
        "child_rhs": gaussian(streams_of[0], (2, 2 * P_SIZE, NRHS), 1.0, 6.0, ((1, 8), (2, 16))),
        "child_inverse_t": gaussian(streams_of[1], (2, 2 * P_SIZE, P_SIZE), (2 * P_SIZE) ** -0.5, 0.046875, ((1, 8), (2, 16))),
        "boundary_tiles": gaussian(streams_of[2], (2, 2 * CB, P_SIZE), (2 * P_SIZE) ** -0.5, 0.046875, ((1, 8), (2, 16))),
        "boundary_lists": draw_boundary_lists(jax.random.fold_in(streams_of[6], 71), 0),
        "root_rhs": gaussian(streams_of[4], (2, R, NRHS), 1.0, 6.0, ((1, 16),)),
        "root_inverse": gaussian(streams_of[5], (2, R, R), (2 * R) ** -0.5, 0.0390625, ((1, 8), (2, 16))),
    }


def turned_dot(left, right):
    return lax.dot_general(left, right, (((0,), (0,)), ((), ())), preferred_element_type=jnp.float32)


def plain_dot(left, right):
    return jnp.dot(left, right, preferred_element_type=jnp.float32)


def reference(child_rhs, child_inverse_t, boundary_tiles, boundary_lists, root_rhs, root_inverse):
    solutions = []
    assembled = jnp.zeros((2, RB, BLK, NRHS), jnp.float32)
    for child in range(2):
        inverse_part = child_inverse_t[:, child * P_SIZE:(child + 1) * P_SIZE, :]
        rhs_part = child_rhs[:, child * P_SIZE:(child + 1) * P_SIZE, :]
        real_part = turned_dot(inverse_part[0], rhs_part[0]) - turned_dot(inverse_part[1], rhs_part[1])
        imag_part = turned_dot(inverse_part[0], rhs_part[1]) + turned_dot(inverse_part[1], rhs_part[0])
        solution = jnp.stack((real_part, imag_part)).astype(jnp.bfloat16)
        solutions.append(solution)
        tiles = boundary_tiles[:, child * CB:(child + 1) * CB, :]
        update_real = plain_dot(tiles[0], solution[0]) - plain_dot(tiles[1], solution[1])
        update_imag = plain_dot(tiles[0], solution[1]) + plain_dot(tiles[1], solution[0])
        update = jnp.stack((update_real, update_imag)).astype(jnp.bfloat16)
        blocks = update.astype(jnp.float32).reshape(2, NBLK, BLK, NRHS)
        assembled = assembled.at[:, boundary_lists[child]].add(blocks)
    root_right = (root_rhs.astype(jnp.float32) - assembled.reshape(2, R, NRHS)).astype(jnp.bfloat16)
    root_real = plain_dot(root_inverse[0], root_right[0]) - plain_dot(root_inverse[1], root_right[1])
    root_imag = plain_dot(root_inverse[0], root_right[1]) + plain_dot(root_inverse[1], root_right[0])
    return jnp.concatenate(solutions, axis=2), jnp.stack((root_real, root_imag))
```

```python
import functools

import jax
import jax.numpy as jnp
from jax import lax
from jax.experimental import pallas as pl
from jax.experimental.pallas import tpu as pltpu
from jax.sharding import PartitionSpec as P

MESH = pl.DeviceIdType.MESH
F32 = jnp.float32
BF16 = jnp.bfloat16
N_SEMS = 128
BLK = 128
TILE = 256


class Wire:
    def __init__(self, send_sems, recv_sems, here):
        self.send_sems, self.recv_sems, self.here = send_sems, recv_sems, here
        self.count = 0
        self.started = []

    def send(self, src, dst, device):
        at = self.count
        self.count += 1
        copy = pltpu.make_async_remote_copy(
            src_ref=src, dst_ref=dst, send_sem=self.send_sems.at[at], recv_sem=self.recv_sems.at[at],
            device_id=device, device_id_type=MESH,
        )
        copy.start()
        self.started.append(copy)
        return at

    def recv(self, at, dst):
        pltpu.make_async_remote_copy(
            src_ref=dst, dst_ref=dst, send_sem=self.send_sems.at[at], recv_sem=self.recv_sems.at[at],
            device_id=self.here, device_id_type=MESH,
        ).wait_recv()

    def drain(self):
        for copy in self.started:
            copy.wait_send()


class Ring:
    def __init__(self, me, up_device, down_device):
        self.me = me
        self.up, self.down, self.far = lax.rem(me + 1, 4), lax.rem(me + 3, 4), lax.rem(me + 2, 4)
        self.up_device, self.down_device = up_device, down_device


class Gather:
    def __init__(self, wire, ring, piece, source=None):
        self.wire, self.ring, self.piece = wire, ring, piece
        self.source = source or (lambda half: piece(half, ring.me))

    def start_half(self, half):
        w, r, piece = self.wire, self.ring, self.piece
        src = self.source(half)
        ahead, behind = (r.up_device, r.down_device) if half == 0 else (r.down_device, r.up_device)
        a = w.send(src, piece(half, r.me), ahead)
        b = w.send(src, piece(half, r.me), behind)
        if half == 0:
            self.a0, self.b0 = a, b
        else:
            self.a1, self.b1 = a, b

    def start(self):
        self.start_half(0)
        self.start_half(1)

    def forward(self):
        w, r, piece = self.wire, self.ring, self.piece
        w.recv(self.a0, piece(0, r.down))
        self.f0 = w.send(piece(0, r.down), piece(0, r.down), r.up_device)
        w.recv(self.a1, piece(1, r.up))
        self.f1 = w.send(piece(1, r.up), piece(1, r.up), r.down_device)

    def finish(self):
        w, r, piece = self.wire, self.ring, self.piece
        w.recv(self.b0, piece(0, r.up))
        w.recv(self.b1, piece(1, r.down))
        w.recv(self.f0, piece(0, r.far))
        w.recv(self.f1, piece(1, r.far))


class Reduce:
    def __init__(self, wire, ring, part, out, first, last):
        self.wire, self.ring, self.part, self.out, self.first, self.last = wire, ring, part, out, first, last

    def start(self):
        w, r, out = self.wire, self.ring, self.out
        out[0] = self.part(0, r.far).astype(BF16)
        self.i0 = w.send(out.at[0], self.first.at[0], r.up_device)
        out[1] = self.part(1, r.far).astype(BF16)
        self.i1 = w.send(out.at[1], self.first.at[1], r.down_device)
        out[2] = self.part(1, r.up).astype(BF16)
        self.i2 = w.send(out.at[2], self.last.at[0], r.up_device)
        out[3] = self.part(0, r.down).astype(BF16)
        self.i3 = w.send(out.at[3], self.last.at[1], r.down_device)

    def middle(self):
        w, r, out = self.wire, self.ring, self.out
        w.recv(self.i0, self.first.at[0])
        out[4] = (self.part(0, r.up) + self.first[0].astype(F32)).astype(BF16)
        self.i4 = w.send(out.at[4], self.last.at[2], r.up_device)
        w.recv(self.i1, self.first.at[1])
        out[5] = (self.part(1, r.down) + self.first[1].astype(F32)).astype(BF16)
        self.i5 = w.send(out.at[5], self.last.at[3], r.down_device)

    def finish(self, half):
        w, r, last = self.wire, self.ring, self.last
        if half == 0:
            w.recv(self.i3, last.at[1])
            w.recv(self.i4, last.at[2])
            return self.part(0, r.me) + last[1].astype(F32) + last[2].astype(F32)
        w.recv(self.i2, last.at[0])
        w.recv(self.i5, last.at[3])
        return self.part(1, r.me) + last[0].astype(F32) + last[3].astype(F32)


def nt_dot(left, right):
    return lax.dot_general(left, right, (((1,), (1,)), ((), ())), preferred_element_type=F32)


def nn_dot(left, right):
    return jnp.dot(left, right, preferred_element_type=F32)


def iota(shape, axis):
    return lax.broadcasted_iota(jnp.int32, shape, axis).astype(F32)


def split_by(value, size):
    quotient = jnp.floor((value + 0.5) * (1.0 / size))
    return quotient, value - quotient * size


def kernel(
    b_ref, a_hbm, f_hbm, lists_ref, rhs_ref, g_hbm, out1_ref, out2_ref,
    a_buf, f_buf, g_buf, b_all, b_neg, b_relay,
    y_part, y_out, y_first, y_last, y_all, y_lhs, y_neg, y_swap,
    u_part, u_out, u_first, u_last, u_own, u_cross, u_relay, u_got, u_flat, u_send,
    s4_in, s4_out, rr, rr_flat, onehot, rhs_t, rhs_send, r_lhs, r_neg,
    v_part, v_out, v_first, v_last, v_own, v_cross, v_relay, v_got,
    send_sems, recv_sems, local_sems,
):
    row, col = lax.axis_index("row"), lax.axis_index("col")
    x_lo, z = lax.div(row, 4), lax.rem(row, 4)
    slot, core = lax.div(col, 2), lax.rem(col, 2)
    x_hi, y = lax.div(slot, 4), lax.rem(slot, 4)
    x = x_hi * 2 + x_lo
    other = 1 - core

    def device(x, y, z, core):
        return (lax.rem(x, 2) * 4 + z, lax.div(x, 2) * 8 + y * 2 + core)

    x_up, x_down = lax.rem(x + 1, 4), lax.rem(x + 3, 4)
    up_x, down_x = device(x_up, y, z, core), device(x_down, y, z, core)
    side_x = device(x_hi * 2 + 1 - x_lo, y, z, core)
    partner = (row, slot * 2 + other)
    y_ring = Ring(y, device(x, lax.rem(y + 1, 4), z, core), device(x, lax.rem(y + 3, 4), z, core))
    z_ring = Ring(z, device(x, y, lax.rem(z + 1, 4), core), device(x, y, lax.rem(z + 3, 4), core))

    def row_peer(step):
        return lax.rem(row + step, 8)

    def slot_peer(step):
        return lax.rem(slot + step, 8)

    own_a = pltpu.make_async_copy(a_hbm, a_buf.at[core], local_sems.at[0])
    own_f = pltpu.make_async_copy(f_hbm, f_buf.at[core], local_sems.at[1])
    own_g = pltpu.make_async_copy(g_hbm, g_buf.at[core], local_sems.at[2])
    own_a.start()

    barrier = pltpu.get_barrier_semaphore()
    greet = [partner, up_x, down_x]
    greet += [(row_peer(step), col) for step in range(1, 8)]
    greet += [(row, slot_peer(step) * 2 + core) for step in range(1, 8)]
    for peer in greet:
        pl.semaphore_signal(barrier, inc=1, device_id=peer, device_id_type=MESH)
    pl.semaphore_wait(barrier, len(greet))

    wire = Wire(send_sems, recv_sems, (row, col))

    def b_piece(x_half):
        return lambda half, place: b_all.at[half, x_half * 4 + place]

    near = Gather(wire, y_ring, b_piece(x_hi), source=lambda half: b_ref.at[half])
    b_x0 = wire.send(b_ref.at[0], b_relay.at[0], up_x)
    b_x1 = wire.send(b_ref.at[1], b_relay.at[1], down_x)
    near.start()
    a_got = wire.send(a_hbm, a_buf.at[core], partner)
    b_all[:, pl.ds(slot, 1)] = b_ref[...].reshape(2, 1, 16, b_ref.shape[2])

    rows, cols = onehot.shape
    t_block, t_rest = split_by(iota((rows, cols), 0), 48)
    t_col, t_at = split_by(t_rest, 12)
    s_chip, s_rest = split_by(iota((rows, cols), 1), 64)
    s_col, _ = split_by(s_rest, 16)
    e_chip, e_rest = split_by(iota((64, cols), 1), 64)
    _, e_at = split_by(e_rest, 16)
    _, e_z = split_by(e_chip, 4)
    spread = (e_z * 16 + e_at == iota((64, cols), 0)).astype(BF16)
    spread_lists = nn_dot(lists_ref[...].astype(F32).astype(BF16), spread)
    source_list = jnp.where(iota((1, cols), 1) < cols // 2, spread_lists[0:1], spread_lists[1:2])
    onehot[...] = jnp.where(
        (t_col == s_col) & (source_list == t_block * 12 + t_at), 1.0, 0.0
    ).astype(BF16)

    pick_slot, pick_rest = split_by(iota((128, 256), 0), 16)
    for mine in (False, True):
        parity = (core if mine else other).astype(F32)
        pick = (pick_slot * 32 + parity * 16 + pick_rest == iota((128, 256), 1)).astype(BF16)
        for plane in range(2):
            turned = nt_dot(pick, rhs_ref[plane]).astype(BF16)
            if mine:
                rhs_t[pl.ds(core, 1), plane] = turned[None]
            else:
                rhs_send[plane] = turned

    own_a.wait()
    own_f.start()

    x_up_hi, x_down_hi = lax.div(x_up, 2), lax.div(x_down, 2)
    wire.recv(b_x0, b_relay.at[0])
    b_x2 = wire.send(b_relay.at[0], b_all.at[0, x_down_hi * 4 + y], up_x)
    wire.recv(b_x1, b_relay.at[1])
    b_x3 = wire.send(b_relay.at[1], b_all.at[1, x_up_hi * 4 + y], down_x)
    near.forward()
    away = Gather(wire, y_ring, b_piece(1 - x_hi))
    wire.recv(b_x2, b_all.at[0, (1 - x_hi) * 4 + y])
    away.start_half(0)
    wire.recv(b_x3, b_all.at[1, (1 - x_hi) * 4 + y])
    away.start_half(1)
    near.finish()
    away.forward()
    away.finish()
    wire.recv(a_got, a_buf.at[other])
    f_got = wire.send(f_hbm, f_buf.at[core], partner)
    rhs_got = wire.send(rhs_send, rhs_t.at[core], partner)
    own_f.wait()
    own_g.start()

    b_neg[0:128] = -b_all[1].reshape(128, b_ref.shape[2])
    b_neg[128:256] = b_all[0].reshape(128, b_ref.shape[2])

    per_q = a_buf.shape[3] // TILE

    def s1_tile(at, carry):
        q, tile = lax.div(at, per_q), lax.rem(at, per_q)
        lanes = pl.ds(pl.multiple_of(tile * TILE, TILE), TILE)
        value = nn_dot(b_all[...].reshape(256, b_ref.shape[2]), a_buf[q, 0, :, lanes])
        value += nn_dot(b_neg[...], a_buf[q, 1, :, lanes])
        where = pl.ds(pl.multiple_of(at * TILE, TILE), TILE)
        y_part[:, :, :, where] = value.reshape(2, 4, 32, TILE)
        return carry

    lax.fori_loop(0, 2 * per_q, s1_tile, 0)

    y_sum = Reduce(wire, z_ring, lambda half, place: y_part[half, place], y_out, y_first, y_last)
    y_sum.start()
    y_sum.middle()
    y_all[0, pl.ds(z, 1)] = y_sum.finish(0).astype(BF16)[None]
    y_gather = Gather(wire, z_ring, lambda half, place: y_all.at[half, place])
    y_gather.start_half(0)
    y_all[1, pl.ds(z, 1)] = y_sum.finish(1).astype(BF16)[None]
    y_gather.start_half(1)
    y_gather.forward()
    y_gather.finish()
    own_cols = pl.ds(pl.multiple_of(core * 512, 512), 512)
    other_cols = pl.ds(pl.multiple_of(other * 512, 512), 512)
    swap_got = wire.send(y_all.at[:, z, :, other_cols], y_swap, partner)
    wire.recv(f_got, f_buf.at[other])
    g_got = wire.send(g_hbm, g_buf.at[core], partner)
    own_g.wait()

    for q in range(2):
        y_re = y_all[0, :, :, q * 512:(q + 1) * 512].reshape(128, 512)
        y_im = y_all[1, :, :, q * 512:(q + 1) * 512].reshape(128, 512)
        y_lhs[q, 0:128] = y_re
        y_lhs[q, 128:256] = y_im
        y_neg[q, 0:128] = -y_im
        y_neg[q, 128:256] = y_re

    def scatter_columns(lhs, neg, weights, part, out, first, last, own, cross, relay, got):
        chunks = part.shape[0]
        tiles = part.shape[-1] // TILE
        sums = []
        for chunk in range(chunks):
            def tile_step(at, carry, chunk=chunk):
                src = pl.ds(pl.multiple_of((chunk * tiles + at) * TILE, TILE), TILE)
                value = nt_dot(lhs[0], weights[0, 0, src, :])
                value += nt_dot(neg[0], weights[0, 1, src, :])
                value += nt_dot(lhs[1], weights[1, 0, src, :])
                value += nt_dot(neg[1], weights[1, 1, src, :])
                where = pl.ds(pl.multiple_of(at * TILE, TILE), TILE)
                part[chunk, :, :, :, :, where] = value.reshape(2, 2, 4, 16, TILE)
                return carry

            lax.fori_loop(0, tiles, tile_step, 0)

            def term(half, place, chunk=chunk):
                return part[chunk, :, (x_hi if half == 1 else 1 - x_hi), place]

            total = Reduce(wire, y_ring, term, out.at[chunk], first.at[chunk], last.at[chunk])
            total.start()
            sums.append(total)
        for total in sums:
            total.middle()
        hops = []
        for chunk, total in enumerate(sums):
            cross[chunk] = total.finish(0).astype(BF16)
            hops.append((
                wire.send(cross.at[chunk, 0], relay.at[chunk, 0], up_x),
                wire.send(cross.at[chunk, 1], relay.at[chunk, 1], down_x),
            ))
        for chunk, total in enumerate(sums):
            own[chunk] = total.finish(1)
        ends = []
        for chunk, (a, b) in enumerate(hops):
            wire.recv(a, relay.at[chunk, 0])
            c = wire.send(relay.at[chunk, 0], got.at[chunk, 0], up_x)
            wire.recv(b, relay.at[chunk, 1])
            d = wire.send(relay.at[chunk, 1], got.at[chunk, 1], down_x)
            ends.append((c, d))
        for chunk, (c, d) in enumerate(ends):
            wire.recv(c, got.at[chunk, 0])
            wire.recv(d, got.at[chunk, 1])
            yield chunk, [own[chunk, plane] + got[chunk, plane].astype(F32) for plane in range(2)]

    for chunk, update in scatter_columns(
        y_lhs, y_neg, f_buf, u_part, u_out, u_first, u_last, u_own, u_cross, u_relay, u_got
    ):
        blocks = u_part.shape[-1] // BLK
        for plane in range(2):
            for block in range(blocks):
                u_flat[plane, pl.ds(chunk * blocks + block, 16, stride=16), :] = (
                    update[plane][:, block * BLK:(block + 1) * BLK]
                )
    u_send[...] = u_flat[...].astype(BF16).reshape(u_send.shape)

    got = []
    for step in range(1, 8):
        to = row_peer(step)
        got.append(wire.send(u_send.at[to], s4_in.at[row], (to, col)))
    s4_in[pl.ds(row, 1)] = u_send[pl.ds(row, 1)]
    for step in range(1, 8):
        wire.recv(got[step - 1], s4_in.at[lax.rem(row + 8 - step, 8)])
    s4_out[...] = nn_dot(onehot[...], s4_in[...].reshape(512, BLK)).astype(BF16).reshape(s4_out.shape)
    got = []
    for step in range(1, 8):
        to = slot_peer(step)
        got.append(wire.send(s4_out.at[to], rr.at[x_lo, slot, z], (row, to * 2 + core)))
    rr[pl.ds(x_lo, 1), pl.ds(slot, 1), pl.ds(z, 1)] = s4_out[pl.ds(slot, 1)].reshape(1, 1, 1, 48, BLK)
    for step in range(1, 8):
        wire.recv(got[step - 1], rr.at[x_lo, lax.rem(slot + 8 - step, 8), z])

    def rr_piece(x_part):
        return lambda half, place: rr.at[x_part, pl.ds(half * 4, 4), place]

    same = Gather(wire, z_ring, rr_piece(x_lo))
    side = Gather(wire, z_ring, rr_piece(1 - x_lo))
    side0 = wire.send(rr.at[x_lo, pl.ds(0, 4), z], rr.at[x_lo, pl.ds(0, 4), z], side_x)
    side1 = wire.send(rr.at[x_lo, pl.ds(4, 4), z], rr.at[x_lo, pl.ds(4, 4), z], side_x)
    same.start()
    wire.recv(side0, rr.at[1 - x_lo, pl.ds(0, 4), z])
    side.start_half(0)
    wire.recv(side1, rr.at[1 - x_lo, pl.ds(4, 4), z])
    side.start_half(1)
    same.forward()
    side.forward()
    same.finish()
    side.finish()

    wire.recv(rhs_got, rhs_t.at[other])
    for plane in range(2):
        rr_flat[plane] = rr[plane].astype(F32).reshape(rr_flat.shape[1:])
        for block in range(12):
            q, lanes = block // 6, slice((block % 6) * BLK, (block % 6 + 1) * BLK)
            assembled = rr_flat[plane, pl.ds(block, 128, stride=12), :]
            right = (rhs_t[q, plane, :, lanes].astype(F32) - assembled).astype(BF16)
            r_lhs[q, plane * 128:(plane + 1) * 128, lanes] = right
            if plane == 0:
                r_neg[q, 128:256, lanes] = right
            else:
                r_neg[q, 0:128, lanes] = -right
    wire.recv(g_got, g_buf.at[other])
    for chunk, root in scatter_columns(
        r_lhs, r_neg, g_buf, v_part, v_out, v_first, v_last, v_own, v_cross, v_relay, v_got
    ):
        width = v_part.shape[-1]
        for plane in range(2):
            out2_ref[plane, :, chunk * width:(chunk + 1) * width] = root[plane]

    wire.recv(swap_got, y_swap)
    for plane in range(2):
        mine = y_all[plane, pl.ds(z, 1), :, own_cols].reshape(32, 512)
        theirs = y_swap[plane]
        for a in range(2):
            rows16 = slice(a * 16, a * 16 + 16)
            out1_ref[plane, pl.ds(pl.multiple_of((2 * a + core) * 16, 16), 16), :] = mine[rows16]
            out1_ref[plane, pl.ds(pl.multiple_of((2 * a + other) * 16, 16), 16), :] = theirs[rows16]
    wire.drain()


def local(child_rhs, child_inverse_t, boundary_tiles, boundary_lists, root_rhs, root_inverse):
    vmem = pltpu.VMEM
    pivots, own_q = child_inverse_t.shape[1], child_inverse_t.shape[2]
    bounds = boundary_tiles.shape[1]
    root_rows, root_cols = root_inverse.shape[1], root_inverse.shape[2]
    whole = pl.BlockSpec(memory_space=pltpu.VMEM)
    far = pl.BlockSpec(memory_space=pl.ANY)

    def scatter_scratch(width, chunks):
        w = width // chunks
        return [
            vmem((chunks, 2, 2, 4, 16, w), F32),
            vmem((chunks, 6, 2, 16, w), BF16),
            vmem((chunks, 2, 2, 16, w), BF16),
            vmem((chunks, 4, 2, 16, w), BF16),
            vmem((chunks, 2, 16, w), F32),
            vmem((chunks, 2, 16, w), BF16),
            vmem((chunks, 2, 16, w), BF16),
            vmem((chunks, 2, 16, w), BF16),
        ]

    scratch = [
        vmem((2, 2, pivots, own_q), BF16),
        vmem((2, 2, bounds, own_q), BF16),
        vmem((2, 2, root_rows, root_cols), BF16),
        vmem((2, 8, 16, pivots), BF16),
        vmem((256, pivots), BF16),
        vmem((2, 16, pivots), BF16),
        vmem((2, 4, 32, 2 * own_q), F32),
        vmem((6, 32, 2 * own_q), BF16),
        vmem((2, 32, 2 * own_q), BF16),
        vmem((4, 32, 2 * own_q), BF16),
        vmem((2, 4, 32, 2 * own_q), BF16),
        vmem((2, 256, own_q), BF16),
        vmem((2, 256, own_q), BF16),
        vmem((2, 32, own_q), BF16),
        *scatter_scratch(bounds, 2),
        vmem((2, 256, BLK), F32),
        vmem((8, 64, BLK), BF16),
        vmem((8, 64, BLK), BF16),
        vmem((8, 48, BLK), BF16),
        vmem((2, 8, 4, 48, BLK), BF16),
        vmem((2, 1536, BLK), F32),
        vmem((384, 512), BF16),
        vmem((2, 2, 128, root_cols), BF16),
        vmem((2, 128, root_cols), BF16),
        vmem((2, 256, root_cols), BF16),
        vmem((2, 256, root_cols), BF16),
        *scatter_scratch(root_rows, 2),
        pltpu.SemaphoreType.DMA((N_SEMS,)),
        pltpu.SemaphoreType.DMA((N_SEMS,)),
        pltpu.SemaphoreType.DMA((3,)),
    ]
    child_t, root_t = pl.pallas_call(
        kernel,
        out_shape=(
            jax.ShapeDtypeStruct((2, 64, own_q), BF16),
            jax.ShapeDtypeStruct((2, 16, root_rows), F32),
        ),
        in_specs=[whole, far, far, whole, whole, far],
        out_specs=(whole, whole),
        scratch_shapes=scratch,
        compiler_params=pltpu.CompilerParams(
            collective_id=0, has_side_effects=True, vmem_limit_bytes=60 * 1024 * 1024
        ),
    )(
        jnp.transpose(child_rhs, (0, 2, 1)), child_inverse_t, boundary_tiles, boundary_lists, root_rhs, root_inverse
    )
    return jnp.transpose(child_t, (0, 2, 1)), jnp.transpose(root_t, (0, 2, 1))


def solution(mesh):
    return jax.shard_map(
        local,
        mesh=mesh,
        in_specs=(
            P(None, "row", "col"),
            P(None, "row", "col"),
            P(None, "row", "col"),
            P(),
            P(None, "col", None),
            P(None, "row", "col"),
        ),
        out_specs=(P(None, "col", "row"), P(None, "row", "col")),
        check_vma=False,
    )
```

```python
import jax
import jax.numpy as jnp
from jax import lax
from jax.experimental import pallas as pl
from jax.experimental.pallas import tpu as pltpu
from jax.sharding import PartitionSpec as P

MESH = pl.DeviceIdType.MESH
F32 = jnp.float32
BF16 = jnp.bfloat16
N_SEMS = 192
BLK = 128
TILE = 256


class Wire:
    def __init__(self, send_sems, recv_sems, here):
        self.send_sems, self.recv_sems, self.here = send_sems, recv_sems, here
        self.count = 0
        self.started = []

    def send(self, src, dst, device):
        at = self.count
        self.count += 1
        copy = pltpu.make_async_remote_copy(
            src_ref=src, dst_ref=dst, send_sem=self.send_sems.at[at], recv_sem=self.recv_sems.at[at],
            device_id=device, device_id_type=MESH,
        )
        copy.start()
        self.started.append(copy)
        return at

    def recv(self, at, dst):
        pltpu.make_async_remote_copy(
            src_ref=dst, dst_ref=dst, send_sem=self.send_sems.at[at], recv_sem=self.recv_sems.at[at],
            device_id=self.here, device_id_type=MESH,
        ).wait_recv()

    def drain(self):
        for copy in self.started:
            copy.wait_send()


class Ring:
    def __init__(self, me, up_device, down_device):
        self.me = me
        self.up, self.down, self.far = lax.rem(me + 1, 4), lax.rem(me + 3, 4), lax.rem(me + 2, 4)
        self.up_device, self.down_device = up_device, down_device


class Gather:
    def __init__(self, wire, ring, piece, source=None):
        self.wire, self.ring, self.piece = wire, ring, piece
        self.source = source or (lambda half: piece(half, ring.me))

    def start_half(self, half):
        w, r, piece = self.wire, self.ring, self.piece
        src = self.source(half)
        ahead, behind = (r.up_device, r.down_device) if half == 0 else (r.down_device, r.up_device)
        a = w.send(src, piece(half, r.me), ahead)
        b = w.send(src, piece(half, r.me), behind)
        if half == 0:
            self.a0, self.b0 = a, b
        else:
            self.a1, self.b1 = a, b

    def start(self):
        self.start_half(0)
        self.start_half(1)

    def forward(self):
        w, r, piece = self.wire, self.ring, self.piece
        w.recv(self.a0, piece(0, r.down))
        self.f0 = w.send(piece(0, r.down), piece(0, r.down), r.up_device)
        w.recv(self.a1, piece(1, r.up))
        self.f1 = w.send(piece(1, r.up), piece(1, r.up), r.down_device)

    def finish(self):
        w, r, piece = self.wire, self.ring, self.piece
        w.recv(self.b0, piece(0, r.up))
        w.recv(self.b1, piece(1, r.down))
        w.recv(self.f0, piece(0, r.far))
        w.recv(self.f1, piece(1, r.far))


class Reduce:
    def __init__(self, wire, ring, part, out, first, last):
        self.wire, self.ring, self.part, self.out, self.first, self.last = wire, ring, part, out, first, last

    def start(self):
        w, r, out = self.wire, self.ring, self.out
        out[0] = self.part(0, r.far).astype(BF16)
        self.i0 = w.send(out.at[0], self.first.at[0], r.up_device)
        out[1] = self.part(1, r.far).astype(BF16)
        self.i1 = w.send(out.at[1], self.first.at[1], r.down_device)
        out[2] = self.part(1, r.up).astype(BF16)
        self.i2 = w.send(out.at[2], self.last.at[0], r.up_device)
        out[3] = self.part(0, r.down).astype(BF16)
        self.i3 = w.send(out.at[3], self.last.at[1], r.down_device)

    def middle(self):
        w, r, out = self.wire, self.ring, self.out
        w.recv(self.i0, self.first.at[0])
        out[4] = (self.part(0, r.up) + self.first[0].astype(F32)).astype(BF16)
        self.i4 = w.send(out.at[4], self.last.at[2], r.up_device)
        w.recv(self.i1, self.first.at[1])
        out[5] = (self.part(1, r.down) + self.first[1].astype(F32)).astype(BF16)
        self.i5 = w.send(out.at[5], self.last.at[3], r.down_device)

    def finish(self, half):
        w, r, last = self.wire, self.ring, self.last
        if half == 0:
            w.recv(self.i3, last.at[1])
            w.recv(self.i4, last.at[2])
            return self.part(0, r.me) + last[1].astype(F32) + last[2].astype(F32)
        w.recv(self.i2, last.at[0])
        w.recv(self.i5, last.at[3])
        return self.part(1, r.me) + last[0].astype(F32) + last[3].astype(F32)


def nt_dot(left, right):
    return lax.dot_general(left, right, (((1,), (1,)), ((), ())), preferred_element_type=F32)


def nn_dot(left, right):
    return jnp.dot(left, right, preferred_element_type=F32)


def iota(shape, axis):
    return lax.broadcasted_iota(jnp.int32, shape, axis).astype(F32)


def split_by(value, size):
    quotient = jnp.floor((value + 0.5) * (1.0 / size))
    return quotient, value - quotient * size


def kernel(
    b_hbm, a_hbm, f_hbm, lists_hbm, rhs_hbm, g_hbm, out1_ref, out2_ref,
    a_buf, f_buf, g_buf, b_all, b_neg,
    y_part, y_out, y_first, y_last, y_all, y_neg, y_swap,
    u_part, u_out, u_first, u_last, u_flat, u_send,
    s4_in, s4_out, rr, rr_flat, onehot, lists_ref, rhs_ref, rhs_t, rhs_send, r_lhs, r_neg,
    v_part, v_out, v_first, v_last, v_own, v_cross, v_got,
    send_sems, recv_sems, local_sems, token_sem,
):
    row, col = lax.axis_index("row"), lax.axis_index("col")
    x_lo, z = lax.div(row, 4), lax.rem(row, 4)
    slot, core = lax.div(col, 2), lax.rem(col, 2)
    x_hi, y = lax.div(slot, 4), lax.rem(slot, 4)
    x = x_hi * 2 + x_lo
    other = 1 - core

    def device(x, y, z, core):
        return (lax.rem(x, 2) * 4 + z, lax.div(x, 2) * 8 + y * 2 + core)

    def place_of(row, slot):
        return (row, slot * 2 + core)

    across = place_of(row, lax.rem(slot + 4, 8))
    side = place_of(lax.rem(row + 4, 8), slot)
    partner = (row, slot * 2 + other)
    y_ring = Ring(y, device(x, lax.rem(y + 1, 4), z, core), device(x, lax.rem(y + 3, 4), z, core))
    z_ring = Ring(z, device(x, y, lax.rem(z + 1, 4), core), device(x, y, lax.rem(z + 3, 4), core))

    barrier = pltpu.get_barrier_semaphore()
    greet = [y_ring.up_device, y_ring.down_device, across, partner, z_ring.up_device, z_ring.down_device, side]
    for peer in greet:
        pl.semaphore_signal(barrier, inc=1, device_id=peer, device_id_type=MESH)

    chunks1, width1 = b_all.shape[0], b_all.shape[4]

    def b_source(chunk, plane):
        return b_hbm.at[plane, :, pl.ds(chunk * width1, width1)]

    fetch = []

    def get(src, dst):
        copy = pltpu.make_async_copy(src, dst, local_sems.at[len(fetch)])
        copy.start()
        fetch.append(copy)
        return copy

    own_b = [
        get(b_source(chunk, plane), b_all.at[chunk, plane, slot]) for chunk in range(chunks1) for plane in range(2)
    ]
    own_lists = get(lists_hbm, lists_ref)
    own_rhs = get(rhs_hbm, rhs_ref)
    own_a = get(a_hbm, a_buf.at[core])
    pl.semaphore_wait(barrier, len(greet))

    wire = Wire(send_sems, recv_sems, (row, col))

    def b_piece(chunk, x_half):
        return lambda half, place: b_all.at[chunk, half, x_half * 4 + place]

    near, away, crossed = [], [], []
    for chunk in range(chunks1):
        crossed.append([
            wire.send(b_source(chunk, plane), b_all.at[chunk, plane, slot], across) for plane in range(2)
        ])
        near.append(Gather(
            wire, y_ring, b_piece(chunk, x_hi), source=lambda half, chunk=chunk: b_source(chunk, half)
        ))
        near[chunk].start()
        away.append(Gather(wire, y_ring, b_piece(chunk, 1 - x_hi)))
    a_got = wire.send(a_hbm, a_buf.at[core], partner)

    own_lists.wait()
    own_rhs.wait()
    cols = onehot.shape[2]
    blocks = u_part.shape[-1] // BLK
    t_block, t_rest = split_by(iota((384, cols), 0), 48)
    t_q, t_rest = split_by(t_rest, 24)
    t_col, t_at = split_by(t_rest, 6)
    s_chip, s_rest = split_by(iota((384, cols), 1), 4 * blocks)
    s_col, _ = split_by(s_rest, blocks)
    e_chip, e_rest = split_by(iota((64, cols), 1), 4 * blocks)
    _, e_at = split_by(e_rest, blocks)
    _, e_z = split_by(e_chip, 4)
    list_values = lists_ref[...].astype(F32).astype(BF16)
    for chunk in range(onehot.shape[0]):
        spread = (e_z * 16 + (chunk * blocks) + e_at == iota((64, cols), 0)).astype(BF16)
        spread_lists = nn_dot(list_values, spread)
        source_list = jnp.where(iota((1, cols), 1) < cols // 2, spread_lists[0:1], spread_lists[1:2])
        onehot[chunk] = jnp.where(
            (t_col == s_col) & (source_list == t_block * 12 + t_q * 6 + t_at), 1.0, 0.0
        ).astype(BF16)

    pick_slot, pick_rest = split_by(iota((128, 256), 0), 16)
    for mine in (False, True):
        parity = (core if mine else other).astype(F32)
        pick = (pick_slot * 32 + parity * 16 + pick_rest == iota((128, 256), 1)).astype(BF16)
        for plane in range(2):
            turned = nt_dot(pick, rhs_ref[plane]).astype(BF16)
            if mine:
                rhs_t[pl.ds(core, 1), plane] = turned[None]
            else:
                rhs_send[plane] = turned

    for chunk in range(chunks1):
        for plane in range(2):
            wire.recv(crossed[chunk][plane], b_all.at[chunk, plane, (1 - x_hi) * 4 + y])
            away[chunk].start_half(plane)
        near[chunk].forward()
    for chunk in range(chunks1):
        away[chunk].forward()
    own_a.wait()
    own_f = get(f_hbm, f_buf.at[core])
    wire.recv(a_got, a_buf.at[other])
    f_got = wire.send(f_hbm, f_buf.at[core], partner)
    rhs_got = wire.send(rhs_send, rhs_t.at[core], partner)

    per_q = a_buf.shape[3] // TILE

    def s1_multiply(chunk, q):
        rows = pl.ds(chunk * width1, width1)

        def tile_step(tile, carry):
            lanes = pl.ds(pl.multiple_of(tile * TILE, TILE), TILE)
            value = nn_dot(b_all[chunk].reshape(256, width1), a_buf[q, 0, rows, lanes])
            value += nn_dot(b_neg[...], a_buf[q, 1, rows, lanes])
            value = value.reshape(2, 4, 32, TILE)
            if chunk > 0:
                value += y_part[q, :, :, :, lanes]
            y_part[q, :, :, :, lanes] = value
            return carry

        lax.fori_loop(0, per_q, tile_step, 0)

    y_sums, y_gathers = [], []
    for q in range(2):
        y_sums.append(Reduce(
            wire, z_ring, lambda half, place, q=q: y_part[q, half, place], y_out.at[q], y_first.at[q], y_last.at[q]
        ))
        y_gathers.append(Gather(wire, z_ring, lambda half, place, q=q: y_all.at[q, half, place]))

    for chunk in range(chunks1):
        near[chunk].finish()
        away[chunk].finish()
        for plane in range(2):
            own_b[chunk * 2 + plane].wait()
        b_neg[0:128] = -b_all[chunk, 1].reshape(128, width1)
        b_neg[128:256] = b_all[chunk, 0].reshape(128, width1)
        for q in range(2):
            s1_multiply(chunk, q)
            if chunk == chunks1 - 1:
                y_sums[q].start()

    for q in range(2):
        y_sums[q].middle()
    for q in range(2):
        for half in range(2):
            y_all[q, half, pl.ds(z, 1)] = y_sums[q].finish(half).astype(BF16)[None]
            y_gathers[q].start_half(half)
    for q in range(2):
        y_gathers[q].forward()
    own_f.wait()
    own_g = get(g_hbm, g_buf.at[core])
    wire.recv(f_got, f_buf.at[other])
    g_got = wire.send(g_hbm, g_buf.at[core], partner)

    def multiply(lhs, neg, weights, q, part, chunk):
        width = part.shape[-1]

        def tile_step(at, carry):
            src = pl.ds(pl.multiple_of(chunk * width + at * TILE, TILE), TILE)
            value = nt_dot(lhs(q), weights[q, 0, src, :])
            value += nt_dot(neg[q], weights[q, 1, src, :])
            value = value.reshape(2, 2, 4, 16, TILE)
            where = pl.ds(pl.multiple_of(at * TILE, TILE), TILE)
            if q > 0:
                value += part[chunk, :, :, :, :, where]
            part[chunk, :, :, :, :, where] = value
            return carry

        lax.fori_loop(0, width // TILE, tile_step, 0)

    def y_reduce(part, out, first, last, chunk):
        def term(half, place):
            return part[chunk, :, (x_hi if half == 1 else 1 - x_hi), place]

        return Reduce(wire, y_ring, term, out.at[chunk], first.at[chunk], last.at[chunk])

    chunks3 = u_part.shape[0]

    def y_lhs(q):
        return y_all[q].reshape(256, y_all.shape[-1])

    u_sums = []
    for q in range(2):
        y_gathers[q].finish()
        if q == 1:
            swap_got = wire.send(y_all.at[other, :, z], y_swap, partner)
        y_neg[q, 0:128] = -y_all[q, 1].reshape(128, y_all.shape[-1])
        y_neg[q, 128:256] = y_all[q, 0].reshape(128, y_all.shape[-1])
        for chunk in range(chunks3):
            multiply(y_lhs, y_neg, f_buf, q, u_part, chunk)
            if q == 1:
                u_sums.append(y_reduce(u_part, u_out, u_first, u_last, chunk))
                u_sums[chunk].start()
    pl.semaphore_signal(token_sem, inc=1, device_id=side, device_id_type=MESH)
    for chunk in range(chunks3):
        u_sums[chunk].middle()

    def s4_peer(half, step):
        return lax.rem(row + step, 8), (slot if half == 1 else lax.rem(slot + 4, 8))

    s4_got = []
    for chunk in range(chunks3):
        for half in range(2):
            update = u_sums[chunk].finish(half)
            for plane in range(2):
                for block in range(blocks):
                    u_flat[plane, pl.ds(block, 16, stride=blocks), :] = update[plane][:, block * BLK:(block + 1) * BLK]
            u_send[chunk, half] = u_flat[...].astype(BF16).reshape(u_send.shape[2:])
            if chunk == 0 and half == 0:
                pl.semaphore_wait(token_sem, 1)
            for step in range(half, 8):
                to_row, to_slot = s4_peer(half, step)
                s4_got.append((chunk, half, step, wire.send(
                    u_send.at[chunk, half, to_row], s4_in.at[chunk, x_hi, row], place_of(to_row, to_slot)
                )))
        s4_in[chunk, pl.ds(x_hi, 1), pl.ds(row, 1)] = u_send[chunk, 1:2, pl.ds(row, 1)]
    for chunk, half, step, at in s4_got:
        wire.recv(at, s4_in.at[chunk, (x_hi if half == 1 else 1 - x_hi), lax.rem(row + 8 - step, 8)])
    total = None
    for chunk in range(chunks3):
        for half in range(2):
            term = nn_dot(onehot[chunk], s4_in[chunk, half].reshape(cols, BLK))
            total = term if total is None else total + term
    s4_out[...] = total.astype(BF16).reshape(s4_out.shape)
    s4_got = []
    for turn in (1, 0):
        to_row = lax.rem(row + 4 * turn, 8)
        for step in range(1 - turn, 8):
            to = lax.rem(slot + step, 8)
            s4_got.append((turn, step, wire.send(s4_out.at[to], rr.at[:, x_lo, slot, z], place_of(to_row, to))))
    rr[:, pl.ds(x_lo, 1), pl.ds(slot, 1), pl.ds(z, 1)] = s4_out[pl.ds(slot, 1)].reshape(2, 1, 1, 1, 24, BLK)
    for turn, step, at in s4_got:
        wire.recv(at, rr.at[:, (1 - x_lo if turn == 1 else x_lo), lax.rem(slot + 8 - step, 8), z])

    r_gathers = [
        Gather(wire, z_ring, lambda half, place, q=q: rr.at[q, half, :, place]) for q in range(2)
    ]
    for q in range(2):
        r_gathers[q].start()
    for q in range(2):
        r_gathers[q].forward()
    own_g.wait()

    def root_lhs(q):
        return r_lhs[q]

    v_sums = []
    chunks5 = v_part.shape[0]
    for q in range(2):
        r_gathers[q].finish()
        if q == 0:
            wire.recv(rhs_got, rhs_t.at[other])
            wire.recv(g_got, g_buf.at[other])
        for plane in range(2):
            rr_flat[...] = rr[q, plane].astype(F32).reshape(rr_flat.shape)
            for block in range(6):
                lanes = slice(block * BLK, (block + 1) * BLK)
                assembled = rr_flat[pl.ds(block, 128, stride=6), :]
                right = (rhs_t[q, plane, :, lanes].astype(F32) - assembled).astype(BF16)
                r_lhs[q, plane * 128:(plane + 1) * 128, lanes] = right
                if plane == 0:
                    r_neg[q, 128:256, lanes] = right
                else:
                    r_neg[q, 0:128, lanes] = -right
        for chunk in range(chunks5):
            multiply(root_lhs, r_neg, g_buf, q, v_part, chunk)
            if q == 1:
                v_sums.append(y_reduce(v_part, v_out, v_first, v_last, chunk))
                v_sums[chunk].start()
    for chunk in range(chunks5):
        v_sums[chunk].middle()
    v_hops = []
    for chunk in range(chunks5):
        v_cross[chunk] = v_sums[chunk].finish(0).astype(BF16)
        v_hops.append(wire.send(v_cross.at[chunk], v_got.at[chunk], across))
    for chunk in range(chunks5):
        v_own[chunk] = v_sums[chunk].finish(1)

    wire.recv(swap_got, y_swap)
    for plane in range(2):
        mine = y_all[pl.ds(core, 1), plane, pl.ds(z, 1)].reshape(32, y_all.shape[-1])
        theirs = y_swap[plane]
        for a in range(2):
            rows16 = slice(a * 16, a * 16 + 16)
            out1_ref[plane, pl.ds(pl.multiple_of((2 * a + core) * 16, 16), 16), :] = mine[rows16]
            out1_ref[plane, pl.ds(pl.multiple_of((2 * a + other) * 16, 16), 16), :] = theirs[rows16]
    width5 = v_part.shape[-1]
    for chunk in range(chunks5):
        wire.recv(v_hops[chunk], v_got.at[chunk])
        out2_ref[:, :, chunk * width5:(chunk + 1) * width5] = v_own[chunk] + v_got[chunk].astype(F32)
    wire.drain()


def copy_out(in1_ref, in2_ref, out1_ref, out2_ref):
    out1_ref[...] = in1_ref[...]
    out2_ref[...] = in2_ref[...]


def local(child_rhs, child_inverse_t, boundary_tiles, boundary_lists, root_rhs, root_inverse):
    vmem = pltpu.VMEM
    pivots, own_q = child_inverse_t.shape[1], child_inverse_t.shape[2]
    bounds = boundary_tiles.shape[1]
    root_rows, root_cols = root_inverse.shape[1], root_inverse.shape[2]
    whole = pl.BlockSpec(memory_space=pltpu.VMEM)
    far = pl.BlockSpec(memory_space=pl.ANY)

    def scatter_scratch(width, chunks):
        w = width // chunks
        return [
            vmem((chunks, 2, 2, 4, 16, w), F32),
            vmem((chunks, 6, 2, 16, w), BF16),
            vmem((chunks, 2, 2, 16, w), BF16),
            vmem((chunks, 4, 2, 16, w), BF16),
        ]

    chunks1, chunks3, chunks5 = 2, 2, 2
    blocks3 = bounds // chunks3 // BLK
    w5 = root_rows // chunks5
    scratch = [
        vmem((2, 2, pivots, own_q), BF16),
        vmem((2, 2, bounds, own_q), BF16),
        vmem((2, 2, root_rows, root_cols), BF16),
        vmem((chunks1, 2, 8, 16, pivots // chunks1), BF16),
        vmem((256, pivots // chunks1), BF16),
        vmem((2, 2, 4, 32, own_q), F32),
        vmem((2, 6, 32, own_q), BF16),
        vmem((2, 2, 32, own_q), BF16),
        vmem((2, 4, 32, own_q), BF16),
        vmem((2, 2, 4, 32, own_q), BF16),
        vmem((2, 256, own_q), BF16),
        vmem((2, 32, own_q), BF16),
        *scatter_scratch(bounds, chunks3),
        vmem((2, 16 * blocks3, BLK), F32),
        vmem((chunks3, 2, 8, 4 * blocks3, BLK), BF16),
        vmem((chunks3, 2, 8, 4 * blocks3, BLK), BF16),
        vmem((8, 2, 24, BLK), BF16),
        vmem((2, 2, 8, 4, 24, BLK), BF16),
        vmem((768, BLK), F32),
        vmem((chunks3, 384, 32 * blocks3), BF16),
        vmem((2, 64), jnp.int32),
        vmem((2, root_cols, 256), BF16),
        vmem((2, 2, 128, root_cols), BF16),
        vmem((2, 128, root_cols), BF16),
        vmem((2, 256, root_cols), BF16),
        vmem((2, 256, root_cols), BF16),
        *scatter_scratch(root_rows, chunks5),
        vmem((chunks5, 2, 16, w5), F32),
        vmem((chunks5, 2, 16, w5), BF16),
        vmem((chunks5, 2, 16, w5), BF16),
        pltpu.SemaphoreType.DMA((N_SEMS,)),
        pltpu.SemaphoreType.DMA((N_SEMS,)),
        pltpu.SemaphoreType.DMA((12,)),
        pltpu.SemaphoreType.REGULAR,
    ]
    shapes = (
        jax.ShapeDtypeStruct((2, 64, own_q), BF16),
        jax.ShapeDtypeStruct((2, 16, root_rows), F32),
    )
    parts = pl.pallas_call(
        kernel,
        out_shape=shapes,
        in_specs=[far] * 6,
        out_specs=(whole, whole),
        scratch_shapes=scratch,
        compiler_params=pltpu.CompilerParams(
            collective_id=0, has_side_effects=True, vmem_limit_bytes=60 * 1024 * 1024
        ),
    )(
        jnp.transpose(child_rhs, (0, 2, 1)), child_inverse_t, boundary_tiles, boundary_lists, root_rhs, root_inverse
    )
    child_t, root_t = pl.pallas_call(
        copy_out, out_shape=shapes, in_specs=[whole, whole], out_specs=(whole, whole),
    )(*parts)
    return jnp.transpose(child_t, (0, 2, 1)), jnp.transpose(root_t, (0, 2, 1))


def solution(mesh):
    return jax.shard_map(
        local,
        mesh=mesh,
        in_specs=(
            P(None, "row", "col"),
            P(None, "row", "col"),
            P(None, "row", "col"),
            P(),
            P(None, "col", None),
            P(None, "row", "col"),
        ),
        out_specs=(P(None, "col", "row"), P(None, "row", "col")),
        check_vma=False,
    )
```

```python
import jax
import jax.numpy as jnp
from jax import lax
from jax.experimental import pallas as pl
from jax.experimental.pallas import tpu as pltpu
from jax.sharding import PartitionSpec as P

MESH = pl.DeviceIdType.MESH
F32 = jnp.float32
BF16 = jnp.bfloat16
N_SENDS, N_RECVS = 96, 121
CROSS, NEAR = 4, 2
BLK = 128
TILE = 256


class Wire:
    def __init__(self, send_sems, recv_sems, group_sends, group_recvs, here):
        self.send_sems, self.recv_sems, self.here = send_sems, recv_sems, here
        self.group_sends, self.group_recvs = group_sends, group_recvs
        self.count = self.high = 0
        self.free = []
        self.started = []

    def copy(self, src, dst, send_sem, recv_sem, device):
        return pltpu.make_async_remote_copy(
            src_ref=src, dst_ref=dst, send_sem=send_sem, recv_sem=recv_sem, device_id=device, device_id_type=MESH
        )

    def send(self, src, dst, device):
        at = self.count
        self.count += 1
        if self.free:
            slot = self.free.pop()
        else:
            slot = self.high
            self.high += 1
        copy = self.copy(src, dst, self.send_sems.at[slot], self.recv_sems.at[at], device)
        copy.start()
        self.started.append((slot, copy))
        return at

    def block(self, many):
        at, slot = self.count, self.high
        self.count += many
        self.high += many
        return at, slot

    def send_block(self, block, step, src, dst, device):
        self.copy(src, dst, self.send_sems.at[block[1] + step], self.recv_sems.at[block[0] + step], device).start()

    def sent_block(self, block, step, src, dst, device):
        at = block[1] + step
        self.started.append(
            (at, self.copy(src, dst, self.send_sems.at[at], self.recv_sems.at[block[0] + step], device))
        )

    def recv(self, at, dst):
        self.copy(dst, dst, self.send_sems.at[0], self.recv_sems.at[at], self.here).wait_recv()

    def recycle(self, keep=0):
        done = self.started[:len(self.started) - keep]
        self.started = self.started[len(done):]
        for slot, copy in done:
            copy.wait_send()
            self.free.append(slot)

    def send_in(self, group, src, dst, device):
        self.copy(src, dst, self.group_sends.at[group], self.group_recvs.at[group], device).start()

    def keep_in(self, group, src, dst):
        pltpu.make_async_copy(src, dst, self.group_recvs.at[group]).start()

    def recv_all(self, group, dst):
        self.copy(dst, dst, self.group_sends.at[group], self.group_recvs.at[group], self.here).wait_recv()

    def sent_all(self, group, src):
        self.copy(src, src, self.group_sends.at[group], self.group_recvs.at[group], self.here).wait_send()


class Ring:
    def __init__(self, me, up_device, down_device, far_device):
        self.me = me
        self.up, self.down, self.far = lax.rem(me + 1, 4), lax.rem(me + 3, 4), lax.rem(me + 2, 4)
        self.up_device, self.down_device, self.far_device = up_device, down_device, far_device


class Gather:
    def __init__(self, wire, ring, piece, source=None):
        self.wire, self.ring, self.piece = wire, ring, piece
        self.source = source or (lambda half: piece(half, ring.me))

    def start_half(self, half):
        w, r, piece = self.wire, self.ring, self.piece
        src = self.source(half)
        ahead, behind = (r.up_device, r.down_device) if half == 0 else (r.down_device, r.up_device)
        a = w.send(src, piece(half, r.me), ahead)
        b = w.send(src, piece(half, r.me), behind)
        if half == 0:
            self.a0, self.b0 = a, b
        else:
            self.a1, self.b1 = a, b

    def start(self):
        self.start_half(0)
        self.start_half(1)

    def forward(self):
        w, r, piece = self.wire, self.ring, self.piece
        w.recv(self.a0, piece(0, r.down))
        self.f0 = w.send(piece(0, r.down), piece(0, r.down), r.up_device)
        w.recv(self.a1, piece(1, r.up))
        self.f1 = w.send(piece(1, r.up), piece(1, r.up), r.down_device)

    def finish(self):
        w, r, piece = self.wire, self.ring, self.piece
        w.recv(self.b0, piece(0, r.up))
        w.recv(self.b1, piece(1, r.down))
        w.recv(self.f0, piece(0, r.far))
        w.recv(self.f1, piece(1, r.far))


class Reduce:
    def __init__(self, wire, ring, chunks, part, out, first, last):
        self.wire, self.ring, self.chunks, self.part = wire, ring, chunks, part
        self.out, self.first, self.last = out, first, last
        self.blocks = [wire.block(chunks) for _ in range(4)]
        self.late = {}

    def early(self, chunk):
        r, out, first, last = self.ring, self.out, self.first, self.last
        return (
            (0, r.far, out.at[chunk, 0], first.at[chunk, 0], r.up_device),
            (1, r.far, out.at[chunk, 1], first.at[chunk, 1], r.down_device),
            (1, r.up, out.at[chunk, 2], last.at[chunk, 0], r.up_device),
            (0, r.down, out.at[chunk, 3], last.at[chunk, 1], r.down_device),
        )

    def start(self, chunk):
        for block, (half, place, src, dst, device) in zip(self.blocks, self.early(chunk)):
            src[...] = self.part(chunk, half, place).astype(BF16)
            self.wire.send_block(block, chunk, src, dst, device)

    def started(self):
        for chunk in range(self.chunks):
            for block, (_, _, src, dst, device) in zip(self.blocks, self.early(chunk)):
                self.wire.sent_block(block, chunk, src, dst, device)

    def middle(self, chunk):
        w, r, out, first, last = self.wire, self.ring, self.out, self.first, self.last
        late = []
        for half, place, device in ((0, r.up, r.up_device), (1, r.down, r.down_device)):
            w.recv(self.blocks[half][0] + chunk, first.at[chunk, half])
            out[chunk, 4 + half] = (self.part(chunk, half, place) + first[chunk, half].astype(F32)).astype(BF16)
            late.append(w.send(out.at[chunk, 4 + half], last.at[chunk, 2 + half], device))
        self.late[chunk] = late

    def finish(self, chunk, half):
        w, last = self.wire, self.last
        w.recv(self.blocks[3 - half][0] + chunk, last.at[chunk, 1 - half])
        w.recv(self.late[chunk][half], last.at[chunk, 2 + half])
        return self.part(chunk, half, self.ring.me) + last[chunk, 1 - half].astype(F32) + last[chunk, 2 + half].astype(F32)


class DirectGather:
    def __init__(self, wire, ring, whole):
        self.wire, self.ring, self.whole = wire, ring, whole

    def start(self):
        w, r, whole = self.wire, self.ring, self.whole
        self.at = [w.send(whole(r.me), whole(r.me), to) for to in (r.far_device, r.up_device, r.down_device)]

    def finish(self):
        r = self.ring
        for at, place in zip(self.at, (r.far, r.down, r.up)):
            self.wire.recv(at, self.whole(place))


class DirectReduce:
    def __init__(self, wire, ring, chunks, part, out, last):
        self.wire, self.ring, self.chunks, self.part = wire, ring, chunks, part
        self.out, self.last = out, last
        self.blocks = [wire.block(chunks) for _ in range(3)]

    def copies(self, chunk):
        r = self.ring
        for at, (place, device) in enumerate(((r.far, r.far_device), (r.up, r.up_device), (r.down, r.down_device))):
            yield at, place, self.out.at[chunk, at], self.last.at[chunk, at], device

    def start(self, chunk):
        for at, place, src, dst, device in self.copies(chunk):
            for half in range(2):
                src[half] = self.part(chunk, half, place).astype(BF16)
            self.wire.send_block(self.blocks[at], chunk, src, dst, device)

    def started(self):
        for chunk in range(self.chunks):
            for at, _, src, dst, device in self.copies(chunk):
                self.wire.sent_block(self.blocks[at], chunk, src, dst, device)

    def middle(self, chunk):
        pass

    def finish(self, chunk, half):
        if half == 0:
            for at in range(3):
                self.wire.recv(self.blocks[at][0] + chunk, self.last.at[chunk, at])
        value = self.part(chunk, half, self.ring.me)
        for at in range(3):
            value = value + self.last[chunk, at, half].astype(F32)
        return value


def nt_dot(left, right):
    return lax.dot_general(left, right, (((1,), (1,)), ((), ())), preferred_element_type=F32)


def nn_dot(left, right):
    return jnp.dot(left, right, preferred_element_type=F32)


def iota(shape, axis):
    return lax.broadcasted_iota(jnp.int32, shape, axis).astype(F32)


def split_by(value, size):
    quotient = jnp.floor((value + 0.5) * (1.0 / size))
    return quotient, value - quotient * size


def kernel(
    b_hbm, a_hbm, f_hbm, lists_hbm, rhs_hbm, g_hbm, out1_ref, out2_ref,
    a_buf, f_buf, g_buf, b_all, b_neg,
    y_part, y_out, y_last, y_all, y_lhs, y_neg, y_swap,
    u_part, u_out, u_first, u_last, u_flat, u_send,
    s4_in, s4_out, rr, rr_flat, onehot, lists_ref, rhs_ref, rhs_t, rhs_send, r_lhs, r_neg,
    v_part, v_out, v_first, v_last, v_own, v_cross, v_got,
    send_sems, recv_sems, group_sends, group_recvs, local_sems, token_sem,
):
    row, col = lax.axis_index("row"), lax.axis_index("col")
    x_lo, z = lax.div(row, 4), lax.rem(row, 4)
    slot, core = lax.div(col, 2), lax.rem(col, 2)
    x_hi, y = lax.div(slot, 4), lax.rem(slot, 4)
    x = x_hi * 2 + x_lo
    other = 1 - core

    def device(x, y, z, core):
        return (lax.rem(x, 2) * 4 + z, lax.div(x, 2) * 8 + y * 2 + core)

    def place_of(row, slot):
        return (row, slot * 2 + core)

    across = place_of(row, lax.rem(slot + 4, 8))
    side = place_of(lax.rem(row + 4, 8), slot)
    partner = (row, slot * 2 + other)
    y_ring = Ring(
        y, device(x, lax.rem(y + 1, 4), z, core), device(x, lax.rem(y + 3, 4), z, core),
        device(x, lax.rem(y + 2, 4), z, core),
    )
    z_ring = Ring(
        z, device(x, y, lax.rem(z + 1, 4), core), device(x, y, lax.rem(z + 3, 4), core),
        device(x, y, lax.rem(z + 2, 4), core),
    )

    barrier = pltpu.get_barrier_semaphore()
    greet = [
        y_ring.up_device, y_ring.down_device, across, partner,
        z_ring.up_device, z_ring.down_device, z_ring.far_device, side,
    ]
    for peer in greet:
        pl.semaphore_signal(barrier, inc=1, device_id=peer, device_id_type=MESH)

    pivots = b_hbm.shape[2]

    def lanes_of(chunk, chunks):
        return pl.ds(chunk * (pivots // chunks), pivots // chunks)

    fetch = []

    def get(src, dst):
        copy = pltpu.make_async_copy(src, dst, local_sems.at[len(fetch)])
        copy.start()
        fetch.append(copy)
        return copy

    own_b = get(b_hbm, b_all.at[:, slot])
    own_lists = get(lists_hbm, lists_ref)
    own_rhs = get(rhs_hbm, rhs_ref)
    own_a = get(a_hbm, a_buf.at[core])
    pl.semaphore_wait(barrier, len(greet))

    wire = Wire(send_sems, recv_sems, group_sends, group_recvs, (row, col))

    def b_piece(chunk, chunks, x_half):
        return lambda half, place: b_all.at[half, x_half * 4 + place, :, lanes_of(chunk, chunks)]

    near, away, crossed = [], [], []
    for chunk in range(CROSS):
        crossed.append(wire.send(
            b_hbm.at[:, :, lanes_of(chunk, CROSS)], b_all.at[:, slot, :, lanes_of(chunk, CROSS)], across
        ))
        away.append(Gather(wire, y_ring, b_piece(chunk, CROSS, 1 - x_hi)))
    for chunk in range(NEAR):
        near.append(Gather(
            wire, y_ring, b_piece(chunk, NEAR, x_hi),
            source=lambda half, chunk=chunk: b_hbm.at[half, :, lanes_of(chunk, NEAR)],
        ))
        near[chunk].start()
    a_got = [wire.send(a_hbm.at[plane], a_buf.at[core, plane], partner) for plane in range(2)]

    own_lists.wait()
    own_rhs.wait()
    cols = onehot.shape[2]
    blocks = u_send.shape[2] // 4
    t_block, t_rest = split_by(iota((384, cols), 0), 48)
    t_q, t_rest = split_by(t_rest, 24)
    t_col, t_at = split_by(t_rest, 6)
    s_chip, s_rest = split_by(iota((384, cols), 1), 4 * blocks)
    s_col, _ = split_by(s_rest, blocks)
    e_chip, e_rest = split_by(iota((64, cols), 1), 4 * blocks)
    _, e_at = split_by(e_rest, blocks)
    _, e_z = split_by(e_chip, 4)
    list_values = lists_ref[...].astype(F32).astype(BF16)
    for chunk in range(onehot.shape[0]):
        spread = (e_z * 16 + (chunk * blocks) + e_at == iota((64, cols), 0)).astype(BF16)
        spread_lists = nn_dot(list_values, spread)
        source_list = jnp.where(iota((1, cols), 1) < cols // 2, spread_lists[0:1], spread_lists[1:2])
        onehot[chunk] = jnp.where(
            (t_col == s_col) & (source_list == t_block * 12 + t_q * 6 + t_at), 1.0, 0.0
        ).astype(BF16)

    pick_slot, pick_rest = split_by(iota((128, 256), 0), 16)
    for mine in (False, True):
        parity = (core if mine else other).astype(F32)
        pick = (pick_slot * 32 + parity * 16 + pick_rest == iota((128, 256), 1)).astype(BF16)
        for plane in range(2):
            turned = nt_dot(pick, rhs_ref[plane]).astype(BF16)
            if mine:
                rhs_t[pl.ds(core, 1), plane] = turned[None]
            else:
                rhs_send[plane] = turned

    for chunk in range(CROSS):
        wire.recv(crossed[chunk], b_all.at[:, (1 - x_hi) * 4 + y, :, lanes_of(chunk, CROSS)])
        away[chunk].start()
        if chunk * NEAR % CROSS == 0:
            near[chunk * NEAR // CROSS].forward()
    for chunk in range(CROSS):
        away[chunk].forward()
    own_a.wait()
    own_f = get(f_hbm, f_buf.at[core])
    for plane in range(2):
        wire.recv(a_got[plane], a_buf.at[other, plane])
    f_got = wire.send(f_hbm, f_buf.at[core], partner)
    rhs_got = wire.send(rhs_send, rhs_t.at[core], partner)
    for gather in near + away:
        gather.finish()
    own_b.wait()

    b_neg[0:128] = -b_all[1].reshape(128, pivots)
    b_neg[128:256] = b_all[0].reshape(128, pivots)
    chunks2, width2 = y_part.shape[0], y_part.shape[-1]
    per_q = chunks2 // 2
    y_sums = DirectReduce(wire, z_ring, chunks2, lambda chunk, half, place: y_part[chunk, half, place], y_out, y_last)
    y_gathers = [
        DirectGather(wire, z_ring, lambda place, chunk=chunk: y_all.at[chunk, :, place]) for chunk in range(chunks2)
    ]

    def s1_step(chunk, carry):
        q = lax.div(chunk, per_q)
        lanes = pl.ds(pl.multiple_of(lax.rem(chunk, per_q) * width2, width2), width2)
        value = nn_dot(b_all[...].reshape(256, pivots), a_buf[q, 0, :, lanes])
        value += nn_dot(b_neg[...], a_buf[q, 1, :, lanes])
        y_part[pl.ds(chunk, 1)] = value.reshape(1, 2, 4, 32, width2)
        y_sums.start(chunk)
        return carry

    lax.fori_loop(0, chunks2, s1_step, 0)
    y_sums.started()

    for chunk in range(chunks2):
        for half in range(2):
            y_all[chunk, half, pl.ds(z, 1)] = y_sums.finish(chunk, half).astype(BF16)[None]
        y_gathers[chunk].start()
    own_f.wait()
    own_g = get(g_hbm, g_buf.at[core])
    wire.recv(f_got, f_buf.at[other])
    wire.recycle(keep=3 * chunks2)
    g_got = wire.send(g_hbm, g_buf.at[core], partner)
    for chunk in range(chunks2):
        y_gathers[chunk].finish()
        q, lanes = chunk // per_q, slice(chunk % per_q * width2, (chunk % per_q + 1) * width2)
        real, imag = y_all[chunk, 0].reshape(128, width2), y_all[chunk, 1].reshape(128, width2)
        y_lhs[q, 0:128, lanes] = real
        y_lhs[q, 128:256, lanes] = imag
        y_neg[q, 0:128, lanes] = -imag
        y_neg[q, 128:256, lanes] = real
    swap_got = wire.send(y_all.at[pl.ds(other * per_q, per_q), :, z], y_swap, partner)

    def multiply(lhs, neg, weights, part, out, first, last):
        chunks, width = part.shape[0], part.shape[-1]

        def term(chunk, half, place):
            return part[chunk, :, (x_hi if half == 1 else 1 - x_hi), place]

        sums = Reduce(wire, y_ring, chunks, term, out, first, last)

        def step(chunk, carry):
            def tile_step(at, carry):
                src = pl.ds(pl.multiple_of(chunk * width + at * TILE, TILE), TILE)
                value = None
                for q in range(2):
                    for left, plane in ((lhs, 0), (neg, 1)):
                        product = nt_dot(left[q], weights[q, plane, src, :])
                        value = product if value is None else value + product
                where = pl.ds(pl.multiple_of(at * TILE, TILE), TILE)
                part[pl.ds(chunk, 1), :, :, :, :, where] = value.reshape(1, 2, 2, 4, 16, TILE)
                return carry

            lax.fori_loop(0, width // TILE, tile_step, 0)
            sums.start(chunk)
            return carry

        lax.fori_loop(0, chunks, step, 0)
        sums.started()
        return sums

    chunks3 = u_part.shape[0]
    u_sums = multiply(y_lhs, y_neg, f_buf, u_part, u_out, u_first, u_last)
    pl.semaphore_signal(token_sem, inc=1, device_id=side, device_id_type=MESH)
    for chunk in range(chunks3):
        u_sums.middle(chunk)

    def s4_peer(half, step):
        return lax.rem(row + step, 8), (slot if half == 1 else lax.rem(slot + 4, 8))

    groups = u_send.shape[0]
    per_group = chunks3 // groups
    width_blocks = blocks // per_group
    for group in range(groups):
        for half in range(2):
            for part in range(per_group):
                update = u_sums.finish(group * per_group + part, half)
                for plane in range(2):
                    for block in range(width_blocks):
                        u_flat[plane, pl.ds(part * width_blocks + block, 16, stride=blocks), :] = (
                            update[plane][:, block * BLK:(block + 1) * BLK]
                        )
            u_send[group, half * 8:half * 8 + 8] = u_flat[...].astype(BF16).reshape(8, 4 * blocks, BLK)
            if group == 0 and half == 0:
                pl.semaphore_wait(token_sem, 1)
            for step in range(half, 8):
                to_row, to_slot = s4_peer(half, step)
                wire.send_in(
                    group, u_send.at[group, half * 8 + to_row], s4_in.at[group, x_hi, row], place_of(to_row, to_slot)
                )
        wire.keep_in(group, u_send.at[group, 8 + row], s4_in.at[group, x_hi, row])
    for group in range(groups):
        wire.recv_all(group, s4_in.at[group])
    total = None
    for group in range(groups):
        for half in range(2):
            term = nn_dot(onehot[group], s4_in[group, half].reshape(cols, BLK))
            total = term if total is None else total + term
    packed = total.astype(BF16).reshape(8, 2, 24, BLK)
    s4_out[0:8] = packed
    s4_out[8:16] = packed
    for turn in (1, 0):
        to_row = lax.rem(row + 4 * turn, 8)
        for step in range(1 - turn, 8):
            to = lax.rem(slot + step, 8)
            wire.send_in(groups, s4_out.at[turn * 8 + to], rr.at[:, x_lo, slot, z], place_of(to_row, to))
    wire.keep_in(groups, s4_out.at[slot], rr.at[:, x_lo, slot, z])
    wire.recv_all(groups, rr.at[:, :, :, z])

    r_gathers = [
        DirectGather(wire, z_ring, lambda place, q=q: rr.at[q, :, :, place]) for q in range(2)
    ]
    for q in range(2):
        r_gathers[q].start()
    own_g.wait()

    chunks5 = v_part.shape[0]
    wire.recv(rhs_got, rhs_t.at[other])
    wire.recv(g_got, g_buf.at[other])
    for q in range(2):
        r_gathers[q].finish()
        for plane in range(2):
            rr_flat[...] = rr[q, plane].astype(F32).reshape(rr_flat.shape)
            for block in range(6):
                lanes = slice(block * BLK, (block + 1) * BLK)
                assembled = rr_flat[pl.ds(block, 128, stride=6), :]
                right = (rhs_t[q, plane, :, lanes].astype(F32) - assembled).astype(BF16)
                r_lhs[q, plane * 128:(plane + 1) * 128, lanes] = right
                if plane == 0:
                    r_neg[q, 128:256, lanes] = right
                else:
                    r_neg[q, 0:128, lanes] = -right
    v_sums = multiply(r_lhs, r_neg, g_buf, v_part, v_out, v_first, v_last)
    for chunk in range(chunks5):
        v_sums.middle(chunk)
    v_hops = []
    for chunk in range(chunks5):
        v_cross[chunk] = v_sums.finish(chunk, 0).astype(BF16)
        v_hops.append(wire.send(v_cross.at[chunk], v_got.at[chunk], across))
    for chunk in range(chunks5):
        v_own[chunk] = v_sums.finish(chunk, 1)

    wire.recv(swap_got, y_swap)
    for at in range(per_q):
        lanes = slice(at * width2, (at + 1) * width2)
        for plane in range(2):
            mine = y_all[pl.ds(core * per_q + at, 1), plane, pl.ds(z, 1)].reshape(32, width2)
            theirs = y_swap[at, plane]
            for a in range(2):
                rows16 = slice(a * 16, a * 16 + 16)
                out1_ref[plane, pl.ds(pl.multiple_of((2 * a + core) * 16, 16), 16), lanes] = mine[rows16]
                out1_ref[plane, pl.ds(pl.multiple_of((2 * a + other) * 16, 16), 16), lanes] = theirs[rows16]
    width5 = v_part.shape[-1]
    for chunk in range(chunks5):
        wire.recv(v_hops[chunk], v_got.at[chunk])
        out2_ref[:, :, chunk * width5:(chunk + 1) * width5] = v_own[chunk] + v_got[chunk].astype(F32)
    wire.recycle()
    for group in range(groups):
        wire.sent_all(group, u_send.at[group, 0:15])
    wire.sent_all(groups, s4_out.at[0:15])


def copy_out(in1_ref, in2_ref, out1_ref, out2_ref):
    out1_ref[...] = in1_ref[...]
    out2_ref[...] = in2_ref[...]


def local(child_rhs, child_inverse_t, boundary_tiles, boundary_lists, root_rhs, root_inverse):
    vmem = pltpu.VMEM
    pivots, own_q = child_inverse_t.shape[1], child_inverse_t.shape[2]
    bounds = boundary_tiles.shape[1]
    root_rows, root_cols = root_inverse.shape[1], root_inverse.shape[2]
    whole = pl.BlockSpec(memory_space=pltpu.VMEM)
    far = pl.BlockSpec(memory_space=pl.ANY)

    def scatter_scratch(width, chunks):
        w = width // chunks
        return [
            vmem((chunks, 2, 2, 4, 16, w), F32),
            vmem((chunks, 6, 2, 16, w), BF16),
            vmem((chunks, 2, 2, 16, w), BF16),
            vmem((chunks, 4, 2, 16, w), BF16),
        ]

    chunks2, chunks3, chunks5, groups = 4, 4, 3, 2
    w2 = 2 * own_q // chunks2
    blocks = bounds // groups // BLK
    w5 = root_rows // chunks5
    scratch = [
        vmem((2, 2, pivots, own_q), BF16),
        vmem((2, 2, bounds, own_q), BF16),
        vmem((2, 2, root_rows, root_cols), BF16),
        vmem((2, 8, 16, pivots), BF16),
        vmem((256, pivots), BF16),
        vmem((chunks2, 2, 4, 32, w2), F32),
        vmem((chunks2, 3, 2, 32, w2), BF16),
        vmem((chunks2, 3, 2, 32, w2), BF16),
        vmem((chunks2, 2, 4, 32, w2), BF16),
        vmem((2, 256, own_q), BF16),
        vmem((2, 256, own_q), BF16),
        vmem((chunks2 // 2, 2, 32, w2), BF16),
        *scatter_scratch(bounds, chunks3),
        vmem((2, 16 * blocks, BLK), F32),
        vmem((groups, 16, 4 * blocks, BLK), BF16),
        vmem((groups, 2, 8, 4 * blocks, BLK), BF16),
        vmem((16, 2, 24, BLK), BF16),
        vmem((2, 2, 8, 4, 24, BLK), BF16),
        vmem((768, BLK), F32),
        vmem((groups, 384, 32 * blocks), BF16),
        vmem((2, 64), jnp.int32),
        vmem((2, root_cols, 256), BF16),
        vmem((2, 2, 128, root_cols), BF16),
        vmem((2, 128, root_cols), BF16),
        vmem((2, 256, root_cols), BF16),
        vmem((2, 256, root_cols), BF16),
        *scatter_scratch(root_rows, chunks5),
        vmem((chunks5, 2, 16, w5), F32),
        vmem((chunks5, 2, 16, w5), BF16),
        vmem((chunks5, 2, 16, w5), BF16),
        pltpu.SemaphoreType.DMA((N_SENDS,)),
        pltpu.SemaphoreType.DMA((N_RECVS,)),
        pltpu.SemaphoreType.DMA((groups + 1,)),
        pltpu.SemaphoreType.DMA((groups + 1,)),
        pltpu.SemaphoreType.DMA((6,)),
        pltpu.SemaphoreType.REGULAR,
    ]
    shapes = (
        jax.ShapeDtypeStruct((2, 64, own_q), BF16),
        jax.ShapeDtypeStruct((2, 16, root_rows), F32),
    )
    parts = pl.pallas_call(
        kernel,
        out_shape=shapes,
        in_specs=[far] * 6,
        out_specs=(whole, whole),
        scratch_shapes=scratch,
        compiler_params=pltpu.CompilerParams(
            collective_id=0, has_side_effects=True, vmem_limit_bytes=60 * 1024 * 1024
        ),
    )(
        jnp.transpose(child_rhs, (0, 2, 1)), child_inverse_t, boundary_tiles, boundary_lists, root_rhs, root_inverse
    )
    child_t, root_t = pl.pallas_call(
        copy_out, out_shape=shapes, in_specs=[whole, whole], out_specs=(whole, whole),
    )(*parts)
    return jnp.transpose(child_t, (0, 2, 1)), jnp.transpose(root_t, (0, 2, 1))


def solution(mesh):
    return jax.shard_map(
        local,
        mesh=mesh,
        in_specs=(
            P(None, "row", "col"),
            P(None, "row", "col"),
            P(None, "row", "col"),
            P(),
            P(None, "col", None),
            P(None, "row", "col"),
        ),
        out_specs=(P(None, "col", "row"), P(None, "row", "col")),
        check_vma=False,
    )
```

```python
import jax
import jax.numpy as jnp
from jax import lax
from jax.experimental import pallas as pl
from jax.experimental.pallas import tpu as pltpu
from jax.sharding import PartitionSpec as P

MESH = pl.DeviceIdType.MESH
F32 = jnp.float32
BF16 = jnp.bfloat16
N_SENDS, N_RECVS = 65, 121
CROSS, NEAR = 4, 2
BLK = 128
TILE = 256


class Wire:
    def __init__(self, send_sems, recv_sems, group_sends, group_recvs, here):
        self.send_sems, self.recv_sems, self.here = send_sems, recv_sems, here
        self.group_sends, self.group_recvs = group_sends, group_recvs
        self.count = self.high = 0
        self.free = []
        self.started = []

    def copy(self, src, dst, send_sem, recv_sem, device):
        return pltpu.make_async_remote_copy(
            src_ref=src, dst_ref=dst, send_sem=send_sem, recv_sem=recv_sem, device_id=device, device_id_type=MESH
        )

    def send(self, src, dst, device):
        at = self.count
        self.count += 1
        if self.free:
            slot = self.free.pop()
        else:
            slot = self.high
            self.high += 1
        copy = self.copy(src, dst, self.send_sems.at[slot], self.recv_sems.at[at], device)
        copy.start()
        self.started.append((slot, copy))
        return at

    def block(self, many):
        at, free = self.count, sorted(self.free)
        self.count += many
        for i in range(len(free) - many + 1):
            if free[i + many - 1] - free[i] == many - 1:
                self.free = free[:i] + free[i + many:]
                return at, free[i]
        slot = self.high
        self.high += many
        return at, slot

    def send_block(self, block, step, src, dst, device):
        self.copy(src, dst, self.send_sems.at[block[1] + step], self.recv_sems.at[block[0] + step], device).start()

    def sent_block(self, block, step, src, dst, device):
        at = block[1] + step
        self.started.append(
            (at, self.copy(src, dst, self.send_sems.at[at], self.recv_sems.at[block[0] + step], device))
        )

    def recv(self, at, dst):
        self.copy(dst, dst, self.send_sems.at[0], self.recv_sems.at[at], self.here).wait_recv()

    def recycle(self, keep=0):
        done = self.started[:len(self.started) - keep]
        self.started = self.started[len(done):]
        for slot, copy in done:
            copy.wait_send()
            self.free.append(slot)

    def send_in(self, group, src, dst, device):
        self.copy(src, dst, self.group_sends.at[group], self.group_recvs.at[group], device).start()

    def keep_in(self, group, src, dst):
        pltpu.make_async_copy(src, dst, self.group_recvs.at[group]).start()

    def recv_all(self, group, dst):
        self.copy(dst, dst, self.group_sends.at[group], self.group_recvs.at[group], self.here).wait_recv()

    def sent_all(self, group, src):
        self.copy(src, src, self.group_sends.at[group], self.group_recvs.at[group], self.here).wait_send()


class Ring:
    def __init__(self, me, up_device, down_device, far_device):
        self.me = me
        self.up, self.down, self.far = lax.rem(me + 1, 4), lax.rem(me + 3, 4), lax.rem(me + 2, 4)
        self.up_device, self.down_device, self.far_device = up_device, down_device, far_device


class Gather:
    def __init__(self, wire, ring, piece, source=None):
        self.wire, self.ring, self.piece = wire, ring, piece
        self.source = source or (lambda half: piece(half, ring.me))

    def start_half(self, half):
        w, r, piece = self.wire, self.ring, self.piece
        src = self.source(half)
        ahead, behind = (r.up_device, r.down_device) if half == 0 else (r.down_device, r.up_device)
        a = w.send(src, piece(half, r.me), ahead)
        b = w.send(src, piece(half, r.me), behind)
        if half == 0:
            self.a0, self.b0 = a, b
        else:
            self.a1, self.b1 = a, b

    def start(self):
        self.start_half(0)
        self.start_half(1)

    def forward(self):
        w, r, piece = self.wire, self.ring, self.piece
        w.recv(self.a0, piece(0, r.down))
        self.f0 = w.send(piece(0, r.down), piece(0, r.down), r.up_device)
        w.recv(self.a1, piece(1, r.up))
        self.f1 = w.send(piece(1, r.up), piece(1, r.up), r.down_device)

    def finish(self):
        w, r, piece = self.wire, self.ring, self.piece
        w.recv(self.b0, piece(0, r.up))
        w.recv(self.b1, piece(1, r.down))
        w.recv(self.f0, piece(0, r.far))
        w.recv(self.f1, piece(1, r.far))


class Reduce:
    def __init__(self, wire, ring, chunks, part, out, first, last):
        self.wire, self.ring, self.chunks, self.part = wire, ring, chunks, part
        self.out, self.first, self.last = out, first, last
        self.blocks = [wire.block(chunks) for _ in range(4)]
        self.late = {}

    def early(self, chunk):
        r, out, first, last = self.ring, self.out, self.first, self.last
        return (
            (0, r.far, out.at[chunk, 0], first.at[chunk, 0], r.up_device),
            (1, r.far, out.at[chunk, 1], first.at[chunk, 1], r.down_device),
            (1, r.up, out.at[chunk, 2], last.at[chunk, 0], r.up_device),
            (0, r.down, out.at[chunk, 3], last.at[chunk, 1], r.down_device),
        )

    def start(self, chunk):
        for block, (half, place, src, dst, device) in zip(self.blocks, self.early(chunk)):
            src[...] = self.part(chunk, half, place).astype(BF16)
            self.wire.send_block(block, chunk, src, dst, device)

    def started(self):
        for chunk in range(self.chunks):
            for block, (_, _, src, dst, device) in zip(self.blocks, self.early(chunk)):
                self.wire.sent_block(block, chunk, src, dst, device)

    def middle(self, chunk):
        w, r, out, first, last = self.wire, self.ring, self.out, self.first, self.last
        late = []
        for half, place, device in ((0, r.up, r.up_device), (1, r.down, r.down_device)):
            w.recv(self.blocks[half][0] + chunk, first.at[chunk, half])
            out[chunk, 4 + half] = (self.part(chunk, half, place) + first[chunk, half].astype(F32)).astype(BF16)
            late.append(w.send(out.at[chunk, 4 + half], last.at[chunk, 2 + half], device))
        self.late[chunk] = late

    def finish(self, chunk, half):
        w, last = self.wire, self.last
        w.recv(self.blocks[3 - half][0] + chunk, last.at[chunk, 1 - half])
        w.recv(self.late[chunk][half], last.at[chunk, 2 + half])
        return self.part(chunk, half, self.ring.me) + last[chunk, 1 - half].astype(F32) + last[chunk, 2 + half].astype(F32)


class DirectGather:
    def __init__(self, wire, ring, whole):
        self.wire, self.ring, self.whole = wire, ring, whole

    def start(self):
        w, r, whole = self.wire, self.ring, self.whole
        self.at = [w.send(whole(r.me), whole(r.me), to) for to in (r.far_device, r.up_device, r.down_device)]

    def finish(self):
        r = self.ring
        for at, place in zip(self.at, (r.far, r.down, r.up)):
            self.wire.recv(at, self.whole(place))


class DirectReduce:
    def __init__(self, wire, ring, chunks, part, out, last):
        self.wire, self.ring, self.chunks, self.part = wire, ring, chunks, part
        self.out, self.last = out, last
        self.blocks = [wire.block(chunks) for _ in range(3)]

    def copies(self, chunk):
        r = self.ring
        for at, (place, device) in enumerate(((r.far, r.far_device), (r.up, r.up_device), (r.down, r.down_device))):
            yield at, place, self.out.at[chunk, at], self.last.at[chunk, at], device

    def start(self, chunk):
        for at, place, src, dst, device in self.copies(chunk):
            for half in range(2):
                src[half] = self.part(chunk, half, place).astype(BF16)
            self.wire.send_block(self.blocks[at], chunk, src, dst, device)

    def started(self):
        for chunk in range(self.chunks):
            for at, _, src, dst, device in self.copies(chunk):
                self.wire.sent_block(self.blocks[at], chunk, src, dst, device)

    def middle(self, chunk):
        pass

    def finish(self, chunk, half):
        if half == 0:
            for at in range(3):
                self.wire.recv(self.blocks[at][0] + chunk, self.last.at[chunk, at])
        value = self.part(chunk, half, self.ring.me)
        for at in range(3):
            value = value + self.last[chunk, at, half].astype(F32)
        return value


def nt_dot(left, right):
    return lax.dot_general(left, right, (((1,), (1,)), ((), ())), preferred_element_type=F32)


def nn_dot(left, right):
    return jnp.dot(left, right, preferred_element_type=F32)


def iota(shape, axis):
    return lax.broadcasted_iota(jnp.int32, shape, axis).astype(F32)


def split_by(value, size):
    quotient = jnp.floor((value + 0.5) * (1.0 / size))
    return quotient, value - quotient * size


def kernel(
    b_hbm, a_hbm, f_hbm, lists_hbm, rhs_hbm, g_hbm, out1_ref, out2_ref,
    a_buf, f_buf, g_buf, b_all, b_neg,
    y_part, y_out, y_last, y_all, y_lhs, y_neg, y_swap,
    u_part, u_out, u_first, u_last, u_flat, u_send,
    s4_in, s4_out, rr, rr_flat, onehot, lists_ref, rhs_ref, rhs_t, rhs_send, r_lhs, r_neg,
    v_part, v_out, v_first, v_last, v_own, v_cross, v_got,
    send_sems, recv_sems, group_sends, group_recvs, local_sems, token_sem,
):
    row, col = lax.axis_index("row"), lax.axis_index("col")
    x_lo, z = lax.div(row, 4), lax.rem(row, 4)
    slot, core = lax.div(col, 2), lax.rem(col, 2)
    x_hi, y = lax.div(slot, 4), lax.rem(slot, 4)
    x = x_hi * 2 + x_lo
    other = 1 - core

    def device(x, y, z, core):
        return (lax.rem(x, 2) * 4 + z, lax.div(x, 2) * 8 + y * 2 + core)

    def place_of(row, slot):
        return (row, slot * 2 + core)

    across = place_of(row, lax.rem(slot + 4, 8))
    side = place_of(lax.rem(row + 4, 8), slot)
    partner = (row, slot * 2 + other)
    y_ring = Ring(
        y, device(x, lax.rem(y + 1, 4), z, core), device(x, lax.rem(y + 3, 4), z, core),
        device(x, lax.rem(y + 2, 4), z, core),
    )
    z_ring = Ring(
        z, device(x, y, lax.rem(z + 1, 4), core), device(x, y, lax.rem(z + 3, 4), core),
        device(x, y, lax.rem(z + 2, 4), core),
    )

    barrier = pltpu.get_barrier_semaphore()
    greet = [
        y_ring.up_device, y_ring.down_device, across, partner,
        z_ring.up_device, z_ring.down_device, z_ring.far_device, side,
    ]
    for peer in greet:
        pl.semaphore_signal(barrier, inc=1, device_id=peer, device_id_type=MESH)

    pivots = b_hbm.shape[2]

    def lanes_of(chunk, chunks):
        return pl.ds(chunk * (pivots // chunks), pivots // chunks)

    fetch = []

    def get(src, dst):
        copy = pltpu.make_async_copy(src, dst, local_sems.at[len(fetch)])
        copy.start()
        fetch.append(copy)
        return copy

    own_b = get(b_hbm, b_all.at[:, slot])
    own_lists = get(lists_hbm, lists_ref)
    own_rhs = get(rhs_hbm, rhs_ref)
    pl.semaphore_wait(barrier, len(greet))
    own_b.wait()

    wire = Wire(send_sems, recv_sems, group_sends, group_recvs, (row, col))

    def b_piece(chunk, chunks, x_half):
        return lambda half, place: b_all.at[half, x_half * 4 + place, :, lanes_of(chunk, chunks)]

    near, away, crossed = [], [], []
    for chunk in range(CROSS):
        crossed.append(wire.send(
            b_all.at[:, slot, :, lanes_of(chunk, CROSS)], b_all.at[:, slot, :, lanes_of(chunk, CROSS)], across
        ))
        away.append(Gather(wire, y_ring, b_piece(chunk, CROSS, 1 - x_hi)))
    for chunk in range(NEAR):
        near.append(Gather(
            wire, y_ring, b_piece(chunk, NEAR, x_hi),
        ))
        near[chunk].start()
    own_a = get(a_hbm, a_buf.at[core])
    a_got = [wire.send(a_hbm.at[plane], a_buf.at[core, plane], partner) for plane in range(2)]

    own_lists.wait()
    own_rhs.wait()
    cols = onehot.shape[2]
    blocks = u_send.shape[2] // 4
    t_block, t_rest = split_by(iota((384, cols), 0), 48)
    t_q, t_rest = split_by(t_rest, 24)
    t_col, t_at = split_by(t_rest, 6)
    s_chip, s_rest = split_by(iota((384, cols), 1), 4 * blocks)
    s_col, _ = split_by(s_rest, blocks)
    e_chip, e_rest = split_by(iota((64, cols), 1), 4 * blocks)
    _, e_at = split_by(e_rest, blocks)
    _, e_z = split_by(e_chip, 4)
    list_values = lists_ref[...].astype(F32).astype(BF16)
    for chunk in range(onehot.shape[0]):
        spread = (e_z * 16 + (chunk * blocks) + e_at == iota((64, cols), 0)).astype(BF16)
        spread_lists = nn_dot(list_values, spread)
        source_list = jnp.where(iota((1, cols), 1) < cols // 2, spread_lists[0:1], spread_lists[1:2])
        onehot[chunk] = jnp.where(
            (t_col == s_col) & (source_list == t_block * 12 + t_q * 6 + t_at), 1.0, 0.0
        ).astype(BF16)

    pick_slot, pick_rest = split_by(iota((128, 256), 0), 16)
    for mine in (False, True):
        parity = (core if mine else other).astype(F32)
        pick = (pick_slot * 32 + parity * 16 + pick_rest == iota((128, 256), 1)).astype(BF16)
        for plane in range(2):
            turned = nt_dot(pick, rhs_ref[plane]).astype(BF16)
            if mine:
                rhs_t[pl.ds(core, 1), plane] = turned[None]
            else:
                rhs_send[plane] = turned

    near[0].forward()
    for chunk in range(CROSS):
        wire.recv(crossed[chunk], b_all.at[:, (1 - x_hi) * 4 + y, :, lanes_of(chunk, CROSS)])
        away[chunk].start()
        if chunk + 1 < NEAR:
            near[chunk + 1].forward()
    for chunk in range(CROSS):
        away[chunk].forward()
    own_a.wait()
    own_f = get(f_hbm, f_buf.at[core])
    for plane in range(2):
        wire.recv(a_got[plane], a_buf.at[other, plane])
    f_got = wire.send(f_hbm, f_buf.at[core], partner)
    rhs_got = wire.send(rhs_send, rhs_t.at[core], partner)
    for gather in near + away:
        gather.finish()
    wire.recycle(keep=2)

    b_neg[0:128] = -b_all[1].reshape(128, pivots)
    b_neg[128:256] = b_all[0].reshape(128, pivots)
    chunks2, width2 = y_part.shape[0], y_part.shape[-1]
    per_q = chunks2 // 2
    y_sums = DirectReduce(wire, z_ring, chunks2, lambda chunk, half, place: y_part[chunk, half, place], y_out, y_last)
    y_gathers = [
        DirectGather(wire, z_ring, lambda place, chunk=chunk: y_all.at[chunk, :, place]) for chunk in range(chunks2)
    ]

    def s1_step(chunk, carry):
        q = lax.div(chunk, per_q)
        lanes = pl.ds(pl.multiple_of(lax.rem(chunk, per_q) * width2, width2), width2)
        value = nn_dot(b_all[...].reshape(256, pivots), a_buf[q, 0, :, lanes])
        value += nn_dot(b_neg[...], a_buf[q, 1, :, lanes])
        y_part[pl.ds(chunk, 1)] = value.reshape(1, 2, 4, 32, width2)
        y_sums.start(chunk)
        return carry

    lax.fori_loop(0, chunks2, s1_step, 0)
    y_sums.started()

    for chunk in range(chunks2):
        for half in range(2):
            y_all[chunk, half, pl.ds(z, 1)] = y_sums.finish(chunk, half).astype(BF16)[None]
        y_gathers[chunk].start()
    own_f.wait()
    own_g = get(g_hbm, g_buf.at[core])
    wire.recv(f_got, f_buf.at[other])
    wire.recycle(keep=3 * chunks2)
    g_got = wire.send(g_hbm, g_buf.at[core], partner)
    for chunk in range(chunks2):
        y_gathers[chunk].finish()
        q, lanes = chunk // per_q, slice(chunk % per_q * width2, (chunk % per_q + 1) * width2)
        real, imag = y_all[chunk, 0].reshape(128, width2), y_all[chunk, 1].reshape(128, width2)
        y_lhs[q, 0:128, lanes] = real
        y_lhs[q, 128:256, lanes] = imag
        y_neg[q, 0:128, lanes] = -imag
        y_neg[q, 128:256, lanes] = real
    swap_got = wire.send(y_all.at[pl.ds(other * per_q, per_q), :, z], y_swap, partner)

    def multiply(lhs, neg, weights, part, out, first, last):
        chunks, width = part.shape[0], part.shape[-1]

        def term(chunk, half, place):
            return part[chunk, :, (x_hi if half == 1 else 1 - x_hi), place]

        sums = Reduce(wire, y_ring, chunks, term, out, first, last)

        def step(chunk, carry):
            def tile_step(at, carry):
                src = pl.ds(pl.multiple_of(chunk * width + at * TILE, TILE), TILE)
                value = None
                for q in range(2):
                    for left, plane in ((lhs, 0), (neg, 1)):
                        product = nt_dot(left[q], weights[q, plane, src, :])
                        value = product if value is None else value + product
                where = pl.ds(pl.multiple_of(at * TILE, TILE), TILE)
                part[pl.ds(chunk, 1), :, :, :, :, where] = value.reshape(1, 2, 2, 4, 16, TILE)
                return carry

            lax.fori_loop(0, width // TILE, tile_step, 0)
            sums.start(chunk)
            return carry

        lax.fori_loop(0, chunks, step, 0)
        sums.started()
        return sums

    chunks3 = u_part.shape[0]
    u_sums = multiply(y_lhs, y_neg, f_buf, u_part, u_out, u_first, u_last)
    pl.semaphore_signal(token_sem, inc=1, device_id=side, device_id_type=MESH)
    for chunk in range(chunks3):
        u_sums.middle(chunk)

    def s4_row(x_step, z_step):
        return lax.rem(x_lo + x_step, 2) * 4 + lax.rem(z + z_step, 4)

    far_first = (2, 1, 3, 0)
    groups = u_send.shape[0]
    per_group = chunks3 // groups
    width_blocks = blocks // per_group
    for group in range(groups):
        for half in range(2):
            for part in range(per_group):
                update = u_sums.finish(group * per_group + part, half)
                for plane in range(2):
                    for block in range(width_blocks):
                        u_flat[plane, pl.ds(part * width_blocks + block, 16, stride=blocks), :] = (
                            update[plane][:, block * BLK:(block + 1) * BLK]
                        )
            u_send[group, half * 8:half * 8 + 8] = u_flat[...].astype(BF16).reshape(8, 4 * blocks, BLK)
            if group == 0 and half == 0:
                pl.semaphore_wait(token_sem, 1)
            to_slot = slot if half == 1 else lax.rem(slot + 4, 8)
            for z_step in far_first:
                for x_step in ((1, 0) if half == 1 else (0, 1)):
                    if half == 1 and x_step == 0 and z_step == 0:
                        continue
                    to_row = s4_row(x_step, z_step)
                    wire.send_in(
                        group, u_send.at[group, half * 8 + to_row], s4_in.at[group, x_hi, row], place_of(to_row, to_slot)
                    )
        wire.keep_in(group, u_send.at[group, 8 + row], s4_in.at[group, x_hi, row])
    for group in range(groups):
        wire.recv_all(group, s4_in.at[group])
    total = None
    for group in range(groups):
        for half in range(2):
            term = nn_dot(onehot[group], s4_in[group, half].reshape(cols, BLK))
            total = term if total is None else total + term
    packed = total.astype(BF16).reshape(8, 2, 24, BLK)
    s4_out[0:8] = packed
    s4_out[8:16] = packed
    for y_step in far_first:
        for half_step, x_step in ((1, 0), (1, 1), (0, 1), (0, 0)):
            if half_step == 0 and x_step == 0 and y_step == 0:
                continue
            to = (x_hi if half_step == 0 else 1 - x_hi) * 4 + lax.rem(y + y_step, 4)
            wire.send_in(
                groups, s4_out.at[x_step * 8 + to], rr.at[:, x_lo, slot, z], place_of(s4_row(x_step, 0), to)
            )
    wire.keep_in(groups, s4_out.at[slot], rr.at[:, x_lo, slot, z])
    wire.recv_all(groups, rr.at[:, :, :, z])

    r_gathers = [
        DirectGather(wire, z_ring, lambda place, q=q: rr.at[q, :, :, place]) for q in range(2)
    ]
    for q in range(2):
        r_gathers[q].start()
    own_g.wait()

    chunks5 = v_part.shape[0]
    wire.recv(rhs_got, rhs_t.at[other])
    wire.recv(g_got, g_buf.at[other])
    for q in range(2):
        r_gathers[q].finish()
        for plane in range(2):
            rr_flat[...] = rr[q, plane].astype(F32).reshape(rr_flat.shape)
            for block in range(6):
                lanes = slice(block * BLK, (block + 1) * BLK)
                assembled = rr_flat[pl.ds(block, 128, stride=6), :]
                right = (rhs_t[q, plane, :, lanes].astype(F32) - assembled).astype(BF16)
                r_lhs[q, plane * 128:(plane + 1) * 128, lanes] = right
                if plane == 0:
                    r_neg[q, 128:256, lanes] = right
                else:
                    r_neg[q, 0:128, lanes] = -right
    v_sums = multiply(r_lhs, r_neg, g_buf, v_part, v_out, v_first, v_last)
    for chunk in range(chunks5):
        v_sums.middle(chunk)
    v_hops = []
    for chunk in range(chunks5):
        v_cross[chunk] = v_sums.finish(chunk, 0).astype(BF16)
        v_hops.append(wire.send(v_cross.at[chunk], v_got.at[chunk], across))
    for chunk in range(chunks5):
        v_own[chunk] = v_sums.finish(chunk, 1)

    wire.recv(swap_got, y_swap)
    for at in range(per_q):
        lanes = slice(at * width2, (at + 1) * width2)
        for plane in range(2):
            mine = y_all[pl.ds(core * per_q + at, 1), plane, pl.ds(z, 1)].reshape(32, width2)
            theirs = y_swap[at, plane]
            for a in range(2):
                rows16 = slice(a * 16, a * 16 + 16)
                out1_ref[plane, pl.ds(pl.multiple_of((2 * a + core) * 16, 16), 16), lanes] = mine[rows16]
                out1_ref[plane, pl.ds(pl.multiple_of((2 * a + other) * 16, 16), 16), lanes] = theirs[rows16]
    width5 = v_part.shape[-1]
    for chunk in range(chunks5):
        wire.recv(v_hops[chunk], v_got.at[chunk])
        out2_ref[:, :, chunk * width5:(chunk + 1) * width5] = v_own[chunk] + v_got[chunk].astype(F32)
    wire.recycle()
    for group in range(groups):
        wire.sent_all(group, u_send.at[group, 0:15])
    wire.sent_all(groups, s4_out.at[0:15])


def local(child_rhs, child_inverse_t, boundary_tiles, boundary_lists, root_rhs, root_inverse):
    vmem = pltpu.VMEM
    pivots, own_q = child_inverse_t.shape[1], child_inverse_t.shape[2]
    bounds = boundary_tiles.shape[1]
    root_rows, root_cols = root_inverse.shape[1], root_inverse.shape[2]
    whole = pl.BlockSpec(memory_space=pltpu.VMEM)
    far = pl.BlockSpec(memory_space=pl.ANY)

    def scatter_scratch(width, chunks):
        w = width // chunks
        return [
            vmem((chunks, 2, 2, 4, 16, w), F32),
            vmem((chunks, 6, 2, 16, w), BF16),
            vmem((chunks, 2, 2, 16, w), BF16),
            vmem((chunks, 4, 2, 16, w), BF16),
        ]

    chunks2, chunks3, chunks5, groups = 4, 4, 3, 2
    w2 = 2 * own_q // chunks2
    blocks = bounds // groups // BLK
    w5 = root_rows // chunks5
    scratch = [
        vmem((2, 2, pivots, own_q), BF16),
        vmem((2, 2, bounds, own_q), BF16),
        vmem((2, 2, root_rows, root_cols), BF16),
        vmem((2, 8, 16, pivots), BF16),
        vmem((256, pivots), BF16),
        vmem((chunks2, 2, 4, 32, w2), F32),
        vmem((chunks2, 3, 2, 32, w2), BF16),
        vmem((chunks2, 3, 2, 32, w2), BF16),
        vmem((chunks2, 2, 4, 32, w2), BF16),
        vmem((2, 256, own_q), BF16),
        vmem((2, 256, own_q), BF16),
        vmem((chunks2 // 2, 2, 32, w2), BF16),
        *scatter_scratch(bounds, chunks3),
        vmem((2, 16 * blocks, BLK), F32),
        vmem((groups, 16, 4 * blocks, BLK), BF16),
        vmem((groups, 2, 8, 4 * blocks, BLK), BF16),
        vmem((16, 2, 24, BLK), BF16),
        vmem((2, 2, 8, 4, 24, BLK), BF16),
        vmem((768, BLK), F32),
        vmem((groups, 384, 32 * blocks), BF16),
        vmem((2, 64), jnp.int32),
        vmem((2, root_cols, 256), BF16),
        vmem((2, 2, 128, root_cols), BF16),
        vmem((2, 128, root_cols), BF16),
        vmem((2, 256, root_cols), BF16),
        vmem((2, 256, root_cols), BF16),
        *scatter_scratch(root_rows, chunks5),
        vmem((chunks5, 2, 16, w5), F32),
        vmem((chunks5, 2, 16, w5), BF16),
        vmem((chunks5, 2, 16, w5), BF16),
        pltpu.SemaphoreType.DMA((N_SENDS,)),
        pltpu.SemaphoreType.DMA((N_RECVS,)),
        pltpu.SemaphoreType.DMA((groups + 1,)),
        pltpu.SemaphoreType.DMA((groups + 1,)),
        pltpu.SemaphoreType.DMA((6,)),
        pltpu.SemaphoreType.REGULAR,
    ]
    shapes = (
        vmem((2, 64, own_q), BF16),
        vmem((2, 16, root_rows), F32),
    )
    child_t, root_t = pl.pallas_call(
        kernel,
        out_shape=shapes,
        in_specs=[far] * 6,
        out_specs=(whole, whole),
        scratch_shapes=scratch,
        compiler_params=pltpu.CompilerParams(
            collective_id=0, has_side_effects=True, vmem_limit_bytes=60 * 1024 * 1024
        ),
    )(
        jnp.transpose(child_rhs, (0, 2, 1)), child_inverse_t, boundary_tiles, boundary_lists, root_rhs, root_inverse
    )
    return jnp.transpose(child_t, (0, 2, 1)), jnp.transpose(root_t, (0, 2, 1))


def solution(mesh):
    return jax.shard_map(
        local,
        mesh=mesh,
        in_specs=(
            P(None, "row", "col"),
            P(None, "row", "col"),
            P(None, "row", "col"),
            P(),
            P(None, "col", None),
            P(None, "row", "col"),
        ),
        out_specs=(P(None, "col", "row"), P(None, "row", "col")),
        check_vma=False,
    )
```

```python
import jax
import jax.numpy as jnp
from jax import lax
from jax.experimental import pallas as pl
from jax.experimental.pallas import tpu as pltpu
from jax.sharding import PartitionSpec as P

MESH = pl.DeviceIdType.MESH
F32 = jnp.float32
BF16 = jnp.bfloat16
N_SENDS, N_RECVS = 55, 100
SPLIT3, SPLIT5 = 3, 2
CROSS, NEAR = 4, 2
BLK = 128
TILE = 256


class Wire:
    def __init__(self, send_sems, recv_sems, group_sends, group_recvs, here):
        self.send_sems, self.recv_sems, self.here = send_sems, recv_sems, here
        self.group_sends, self.group_recvs = group_sends, group_recvs
        self.count = self.high = 0
        self.free = []
        self.started = []

    def copy(self, src, dst, send_sem, recv_sem, device):
        return pltpu.make_async_remote_copy(
            src_ref=src, dst_ref=dst, send_sem=send_sem, recv_sem=recv_sem, device_id=device, device_id_type=MESH
        )

    def send(self, src, dst, device):
        at = self.count
        self.count += 1
        if self.free:
            slot = self.free.pop()
        else:
            slot = self.high
            self.high += 1
        copy = self.copy(src, dst, self.send_sems.at[slot], self.recv_sems.at[at], device)
        copy.start()
        self.started.append((slot, copy))
        return at

    def block(self, many):
        at, free = self.count, sorted(self.free)
        self.count += many
        for i in range(len(free) - many + 1):
            if free[i + many - 1] - free[i] == many - 1:
                self.free = free[:i] + free[i + many:]
                return at, free[i]
        slot = self.high
        self.high += many
        return at, slot

    def send_block(self, block, step, src, dst, device):
        self.copy(src, dst, self.send_sems.at[block[1] + step], self.recv_sems.at[block[0] + step], device).start()

    def sent_block(self, block, step, src, dst, device):
        at = block[1] + step
        self.started.append(
            (at, self.copy(src, dst, self.send_sems.at[at], self.recv_sems.at[block[0] + step], device))
        )

    def recv(self, at, dst):
        self.copy(dst, dst, self.send_sems.at[0], self.recv_sems.at[at], self.here).wait_recv()

    def recycle(self, keep=0):
        done = self.started[:len(self.started) - keep]
        self.started = self.started[len(done):]
        for slot, copy in done:
            copy.wait_send()
            self.free.append(slot)

    def send_in(self, group, src, dst, device):
        self.copy(src, dst, self.group_sends.at[group], self.group_recvs.at[group], device).start()

    def keep_in(self, group, src, dst):
        pltpu.make_async_copy(src, dst, self.group_recvs.at[group]).start()

    def recv_all(self, group, dst):
        self.copy(dst, dst, self.group_sends.at[group], self.group_recvs.at[group], self.here).wait_recv()

    def sent_all(self, group, src):
        self.copy(src, src, self.group_sends.at[group], self.group_recvs.at[group], self.here).wait_send()


class Ring:
    def __init__(self, me, up_device, down_device, far_device):
        self.me = me
        self.up, self.down, self.far = lax.rem(me + 1, 4), lax.rem(me + 3, 4), lax.rem(me + 2, 4)
        self.up_device, self.down_device, self.far_device = up_device, down_device, far_device


class Gather:
    def __init__(self, wire, ring, piece, source=None):
        self.wire, self.ring, self.piece = wire, ring, piece
        self.source = source or (lambda half: piece(half, ring.me))

    def start_half(self, half):
        w, r, piece = self.wire, self.ring, self.piece
        src = self.source(half)
        ahead, behind = (r.up_device, r.down_device) if half == 0 else (r.down_device, r.up_device)
        a = w.send(src, piece(half, r.me), ahead)
        b = w.send(src, piece(half, r.me), behind)
        if half == 0:
            self.a0, self.b0 = a, b
        else:
            self.a1, self.b1 = a, b

    def start(self):
        self.start_half(0)
        self.start_half(1)

    def forward(self):
        w, r, piece = self.wire, self.ring, self.piece
        w.recv(self.a0, piece(0, r.down))
        self.f0 = w.send(piece(0, r.down), piece(0, r.down), r.up_device)
        w.recv(self.a1, piece(1, r.up))
        self.f1 = w.send(piece(1, r.up), piece(1, r.up), r.down_device)

    def finish(self):
        w, r, piece = self.wire, self.ring, self.piece
        w.recv(self.b0, piece(0, r.up))
        w.recv(self.b1, piece(1, r.down))
        w.recv(self.f0, piece(0, r.far))
        w.recv(self.f1, piece(1, r.far))


class Reduce:
    def __init__(self, wire, ring, chunks, part, out, first, last):
        self.wire, self.ring, self.chunks, self.part = wire, ring, chunks, part
        self.out, self.first, self.last = out, first, last
        self.blocks = [wire.block(chunks) for _ in range(4)]
        self.late = {}

    def early(self, chunk):
        r, out, first, last = self.ring, self.out, self.first, self.last
        return (
            (0, r.far, out.at[chunk, 0], first.at[chunk, 0], r.up_device),
            (1, r.far, out.at[chunk, 1], first.at[chunk, 1], r.down_device),
            (1, r.up, out.at[chunk, 2], last.at[chunk, 0], r.up_device),
            (0, r.down, out.at[chunk, 3], last.at[chunk, 1], r.down_device),
        )

    def start(self, chunk):
        for block, (half, place, src, dst, device) in zip(self.blocks, self.early(chunk)):
            src[...] = self.part(chunk, half, place).astype(BF16)
            self.wire.send_block(block, chunk, src, dst, device)

    def started(self):
        for chunk in range(self.chunks):
            for block, (_, _, src, dst, device) in zip(self.blocks, self.early(chunk)):
                self.wire.sent_block(block, chunk, src, dst, device)

    def middle(self, chunk):
        w, r, out, first, last = self.wire, self.ring, self.out, self.first, self.last
        late = []
        for half, place, device in ((0, r.up, r.up_device), (1, r.down, r.down_device)):
            w.recv(self.blocks[half][0] + chunk, first.at[chunk, half])
            out[chunk, 4 + half] = (self.part(chunk, half, place) + first[chunk, half].astype(F32)).astype(BF16)
            late.append(w.send(out.at[chunk, 4 + half], last.at[chunk, 2 + half], device))
        self.late[chunk] = late

    def finish(self, chunk, half):
        w, last = self.wire, self.last
        w.recv(self.blocks[3 - half][0] + chunk, last.at[chunk, 1 - half])
        w.recv(self.late[chunk][half], last.at[chunk, 2 + half])
        return self.part(chunk, half, self.ring.me) + last[chunk, 1 - half].astype(F32) + last[chunk, 2 + half].astype(F32)


class DirectGather:
    def __init__(self, wire, ring, whole):
        self.wire, self.ring, self.whole = wire, ring, whole

    def start(self):
        w, r, whole = self.wire, self.ring, self.whole
        self.at = [w.send(whole(r.me), whole(r.me), to) for to in (r.far_device, r.up_device, r.down_device)]

    def finish(self):
        r = self.ring
        for at, place in zip(self.at, (r.far, r.down, r.up)):
            self.wire.recv(at, self.whole(place))


class DirectReduce:
    def __init__(self, wire, ring, chunks, part, out, last):
        self.wire, self.ring, self.chunks, self.part = wire, ring, chunks, part
        self.out, self.last = out, last
        self.block = wire.block(chunks)

    def copies(self, chunk):
        r = self.ring
        for at, (place, device) in enumerate(((r.far, r.far_device), (r.up, r.up_device), (r.down, r.down_device))):
            yield at, place, self.out.at[chunk, at], self.last.at[chunk, at], device

    def start(self, chunk):
        for at, place, src, dst, device in self.copies(chunk):
            for half in range(2):
                src[half] = self.part(chunk, half, place).astype(BF16)
            self.wire.send_block(self.block, chunk, src, dst, device)

    def started(self):
        for chunk in range(self.chunks):
            self.wire.sent_block(self.block, chunk, self.out.at[chunk], self.last.at[chunk], self.wire.here)

    def middle(self, chunk):
        pass

    def finish(self, chunk, half):
        if half == 0:
            self.wire.recv(self.block[0] + chunk, self.last.at[chunk])
        value = self.part(chunk, half, self.ring.me)
        for at in range(3):
            value = value + self.last[chunk, at, half].astype(F32)
        return value


class Mixed:
    def __init__(self, relayed, direct, split):
        self.relayed, self.direct, self.split = relayed, direct, split

    def middle(self, chunk):
        if chunk < self.split:
            self.relayed.middle(chunk)

    def finish(self, chunk, half):
        if chunk < self.split:
            return self.relayed.finish(chunk, half)
        return self.direct.finish(chunk - self.split, half)


def nt_dot(left, right):
    return lax.dot_general(left, right, (((1,), (1,)), ((), ())), preferred_element_type=F32)


def nn_dot(left, right):
    return jnp.dot(left, right, preferred_element_type=F32)


def iota(shape, axis):
    return lax.broadcasted_iota(jnp.int32, shape, axis).astype(F32)


def split_by(value, size):
    quotient = jnp.floor((value + 0.5) * (1.0 / size))
    return quotient, value - quotient * size


def kernel(
    b_hbm, a_hbm, f_hbm, lists_hbm, rhs_hbm, g_hbm, out1_ref, out2_ref,
    a_buf, f_buf, g_buf, b_all, b_neg,
    y_part, y_out, y_last, y_all, y_lhs, y_neg, y_swap,
    u_part, u_out, u_first, u_last, u_dout, u_dlast, u_flat, u_send,
    s4_in, s4_out, rr, rr_flat, onehot, lists_ref, rhs_ref, rhs_t, rhs_send, r_lhs, r_neg,
    v_part, v_out, v_first, v_last, v_dout, v_dlast, v_own, v_cross, v_got,
    send_sems, recv_sems, group_sends, group_recvs, local_sems, token_sem,
):
    row, col = lax.axis_index("row"), lax.axis_index("col")
    x_lo, z = lax.div(row, 4), lax.rem(row, 4)
    slot, core = lax.div(col, 2), lax.rem(col, 2)
    x_hi, y = lax.div(slot, 4), lax.rem(slot, 4)
    x = x_hi * 2 + x_lo
    other = 1 - core

    def device(x, y, z, core):
        return (lax.rem(x, 2) * 4 + z, lax.div(x, 2) * 8 + y * 2 + core)

    def place_of(row, slot):
        return (row, slot * 2 + core)

    across = place_of(row, lax.rem(slot + 4, 8))
    side = place_of(lax.rem(row + 4, 8), slot)
    partner = (row, slot * 2 + other)
    y_ring = Ring(
        y, device(x, lax.rem(y + 1, 4), z, core), device(x, lax.rem(y + 3, 4), z, core),
        device(x, lax.rem(y + 2, 4), z, core),
    )
    z_ring = Ring(
        z, device(x, y, lax.rem(z + 1, 4), core), device(x, y, lax.rem(z + 3, 4), core),
        device(x, y, lax.rem(z + 2, 4), core),
    )

    barrier = pltpu.get_barrier_semaphore()
    greet = [
        y_ring.up_device, y_ring.down_device, across, partner,
        z_ring.up_device, z_ring.down_device, z_ring.far_device, side,
    ]
    for peer in greet:
        pl.semaphore_signal(barrier, inc=1, device_id=peer, device_id_type=MESH)

    pivots = b_hbm.shape[2]

    def lanes_of(chunk, chunks):
        return pl.ds(chunk * (pivots // chunks), pivots // chunks)

    fetch = []

    def get(src, dst):
        copy = pltpu.make_async_copy(src, dst, local_sems.at[len(fetch)])
        copy.start()
        fetch.append(copy)
        return copy

    own_b = get(b_hbm, b_all.at[:, slot])
    own_lists = get(lists_hbm, lists_ref)
    own_rhs = get(rhs_hbm, rhs_ref)
    pl.semaphore_wait(barrier, len(greet))
    own_b.wait()

    wire = Wire(send_sems, recv_sems, group_sends, group_recvs, (row, col))

    def b_piece(chunk, chunks, x_half):
        return lambda half, place: b_all.at[half, x_half * 4 + place, :, lanes_of(chunk, chunks)]

    near, away, crossed = [], [], []
    for chunk in range(CROSS):
        crossed.append(wire.send(
            b_all.at[:, slot, :, lanes_of(chunk, CROSS)], b_all.at[:, slot, :, lanes_of(chunk, CROSS)], across
        ))
        if chunk < CROSS - 1:
            away.append(Gather(wire, y_ring, b_piece(chunk, CROSS, 1 - x_hi)))
        else:
            away.append(DirectGather(
                wire, y_ring, lambda place, chunk=chunk: b_all.at[:, (1 - x_hi) * 4 + place, :, lanes_of(chunk, CROSS)]
            ))
    for chunk in range(NEAR):
        near.append(Gather(
            wire, y_ring, b_piece(chunk, NEAR, x_hi),
        ))
        near[chunk].start()
    own_a = get(a_hbm, a_buf.at[core])
    a_got = [wire.send(a_hbm.at[plane], a_buf.at[core, plane], partner) for plane in range(2)]

    own_lists.wait()
    own_rhs.wait()
    cols = onehot.shape[2]
    blocks = u_send.shape[2] // 4
    t_block, t_rest = split_by(iota((384, cols), 0), 48)
    t_q, t_rest = split_by(t_rest, 24)
    t_col, t_at = split_by(t_rest, 6)
    s_chip, s_rest = split_by(iota((384, cols), 1), 4 * blocks)
    s_col, _ = split_by(s_rest, blocks)
    e_chip, e_rest = split_by(iota((64, cols), 1), 4 * blocks)
    _, e_at = split_by(e_rest, blocks)
    _, e_z = split_by(e_chip, 4)
    list_values = lists_ref[...].astype(F32).astype(BF16)
    for chunk in range(onehot.shape[0]):
        spread = (e_z * 16 + (chunk * blocks) + e_at == iota((64, cols), 0)).astype(BF16)
        spread_lists = nn_dot(list_values, spread)
        source_list = jnp.where(iota((1, cols), 1) < cols // 2, spread_lists[0:1], spread_lists[1:2])
        onehot[chunk] = jnp.where(
            (t_col == s_col) & (source_list == t_block * 12 + t_q * 6 + t_at), 1.0, 0.0
        ).astype(BF16)

    pick_slot, pick_rest = split_by(iota((128, 256), 0), 16)
    for mine in (False, True):
        parity = (core if mine else other).astype(F32)
        pick = (pick_slot * 32 + parity * 16 + pick_rest == iota((128, 256), 1)).astype(BF16)
        for plane in range(2):
            turned = nt_dot(pick, rhs_ref[plane]).astype(BF16)
            if mine:
                rhs_t[pl.ds(core, 1), plane] = turned[None]
            else:
                rhs_send[plane] = turned

    near[0].forward()
    for chunk in range(CROSS):
        wire.recv(crossed[chunk], b_all.at[:, (1 - x_hi) * 4 + y, :, lanes_of(chunk, CROSS)])
        away[chunk].start()
        if chunk + 1 < NEAR:
            near[chunk + 1].forward()
    for chunk in range(CROSS - 1):
        away[chunk].forward()
    own_a.wait()
    own_f = get(f_hbm, f_buf.at[core])
    for plane in range(2):
        wire.recv(a_got[plane], a_buf.at[other, plane])
    f_got = wire.send(f_hbm, f_buf.at[core], partner)
    rhs_got = wire.send(rhs_send, rhs_t.at[core], partner)
    for gather in near + away:
        gather.finish()
    wire.recycle(keep=2)

    b_neg[0:128] = -b_all[1].reshape(128, pivots)
    b_neg[128:256] = b_all[0].reshape(128, pivots)
    chunks2, width2 = y_part.shape[0], y_part.shape[-1]
    per_q = chunks2 // 2
    y_sums = DirectReduce(wire, z_ring, chunks2, lambda chunk, half, place: y_part[chunk, half, place], y_out, y_last)
    y_gathers = [
        DirectGather(wire, z_ring, lambda place, chunk=chunk: y_all.at[chunk, :, place]) for chunk in range(chunks2)
    ]

    def s1_step(chunk, carry):
        q = lax.div(chunk, per_q)
        lanes = pl.ds(pl.multiple_of(lax.rem(chunk, per_q) * width2, width2), width2)
        value = nn_dot(b_all[...].reshape(256, pivots), a_buf[q, 0, :, lanes])
        value += nn_dot(b_neg[...], a_buf[q, 1, :, lanes])
        y_part[pl.ds(chunk, 1)] = value.reshape(1, 2, 4, 32, width2)
        y_sums.start(chunk)
        return carry

    lax.fori_loop(0, chunks2, s1_step, 0)
    y_sums.started()

    for chunk in range(chunks2):
        for half in range(2):
            y_all[chunk, half, pl.ds(z, 1)] = y_sums.finish(chunk, half).astype(BF16)[None]
        y_gathers[chunk].start()
    own_f.wait()
    own_g = get(g_hbm, g_buf.at[core])
    wire.recv(f_got, f_buf.at[other])
    wire.recycle(keep=3 * chunks2)
    g_got = wire.send(g_hbm, g_buf.at[core], partner)
    for chunk in range(chunks2):
        y_gathers[chunk].finish()
        q, lanes = chunk // per_q, slice(chunk % per_q * width2, (chunk % per_q + 1) * width2)
        real, imag = y_all[chunk, 0].reshape(128, width2), y_all[chunk, 1].reshape(128, width2)
        y_lhs[q, 0:128, lanes] = real
        y_lhs[q, 128:256, lanes] = imag
        y_neg[q, 0:128, lanes] = -imag
        y_neg[q, 128:256, lanes] = real
    swap_got = wire.send(y_all.at[pl.ds(other * per_q, per_q), :, z], y_swap, partner)

    def multiply(lhs, neg, weights, part, out, first, last, direct_out, direct_last):
        chunks, width, split = part.shape[0], part.shape[-1], out.shape[0]

        def term(chunk, half, place):
            return part[chunk, :, (x_hi if half == 1 else 1 - x_hi), place]

        relayed = Reduce(wire, y_ring, split, term, out, first, last)
        direct = DirectReduce(
            wire, y_ring, chunks - split, lambda chunk, half, place: term(chunk + split, half, place),
            direct_out, direct_last,
        )

        def product(chunk):
            def tile_step(at, carry):
                src = pl.ds(pl.multiple_of(chunk * width + at * TILE, TILE), TILE)
                value = None
                for q in range(2):
                    for left, plane in ((lhs, 0), (neg, 1)):
                        product = nt_dot(left[q], weights[q, plane, src, :])
                        value = product if value is None else value + product
                where = pl.ds(pl.multiple_of(at * TILE, TILE), TILE)
                part[pl.ds(chunk, 1), :, :, :, :, where] = value.reshape(1, 2, 2, 4, 16, TILE)
                return carry

            lax.fori_loop(0, width // TILE, tile_step, 0)

        def relayed_step(chunk, carry):
            product(chunk)
            relayed.start(chunk)
            return carry

        def direct_step(chunk, carry):
            product(chunk + split)
            direct.start(chunk)
            return carry

        lax.fori_loop(0, split, relayed_step, 0)
        lax.fori_loop(0, chunks - split, direct_step, 0)
        relayed.started()
        direct.started()
        return Mixed(relayed, direct, split)

    chunks3 = u_part.shape[0]
    u_sums = multiply(y_lhs, y_neg, f_buf, u_part, u_out, u_first, u_last, u_dout, u_dlast)
    pl.semaphore_signal(token_sem, inc=1, device_id=side, device_id_type=MESH)
    for chunk in range(chunks3):
        u_sums.middle(chunk)

    def s4_row(x_step, z_step):
        return lax.rem(x_lo + x_step, 2) * 4 + lax.rem(z + z_step, 4)

    far_first = (2, 1, 3, 0)
    groups = u_send.shape[0]
    per_group = chunks3 // groups
    width_blocks = blocks // per_group
    for group in range(groups):
        for half in range(2):
            for part in range(per_group):
                update = u_sums.finish(group * per_group + part, half)
                for plane in range(2):
                    for block in range(width_blocks):
                        u_flat[plane, pl.ds(part * width_blocks + block, 16, stride=blocks), :] = (
                            update[plane][:, block * BLK:(block + 1) * BLK]
                        )
            u_send[group, half * 8:half * 8 + 8] = u_flat[...].astype(BF16).reshape(8, 4 * blocks, BLK)
            if group == 0 and half == 0:
                pl.semaphore_wait(token_sem, 1)
            to_slot = slot if half == 1 else lax.rem(slot + 4, 8)
            for z_step in far_first:
                for x_step in ((1, 0) if half == 1 else (0, 1)):
                    if half == 1 and x_step == 0 and z_step == 0:
                        continue
                    to_row = s4_row(x_step, z_step)
                    wire.send_in(
                        group, u_send.at[group, half * 8 + to_row], s4_in.at[group, x_hi, row], place_of(to_row, to_slot)
                    )
        wire.keep_in(group, u_send.at[group, 8 + row], s4_in.at[group, x_hi, row])
    for group in range(groups):
        wire.recv_all(group, s4_in.at[group])
    total = None
    for group in range(groups):
        for half in range(2):
            term = nn_dot(onehot[group], s4_in[group, half].reshape(cols, BLK))
            total = term if total is None else total + term
    packed = total.astype(BF16).reshape(8, 2, 24, BLK)
    s4_out[0:8] = packed
    s4_out[8:16] = packed
    for y_step in far_first:
        for half_step, x_step in ((1, 0), (1, 1), (0, 1), (0, 0)):
            if half_step == 0 and x_step == 0 and y_step == 0:
                continue
            to = (x_hi if half_step == 0 else 1 - x_hi) * 4 + lax.rem(y + y_step, 4)
            wire.send_in(
                groups, s4_out.at[x_step * 8 + to], rr.at[:, x_lo, slot, z], place_of(s4_row(x_step, 0), to)
            )
    wire.keep_in(groups, s4_out.at[slot], rr.at[:, x_lo, slot, z])
    wire.recv_all(groups, rr.at[:, :, :, z])

    r_gathers = [
        DirectGather(wire, z_ring, lambda place, q=q: rr.at[q, :, :, place]) for q in range(2)
    ]
    for q in range(2):
        r_gathers[q].start()
    own_g.wait()

    chunks5 = v_part.shape[0]
    wire.recv(rhs_got, rhs_t.at[other])
    wire.recv(g_got, g_buf.at[other])
    for q in range(2):
        r_gathers[q].finish()
        for plane in range(2):
            rr_flat[...] = rr[q, plane].astype(F32).reshape(rr_flat.shape)
            for block in range(6):
                lanes = slice(block * BLK, (block + 1) * BLK)
                assembled = rr_flat[pl.ds(block, 128, stride=6), :]
                right = (rhs_t[q, plane, :, lanes].astype(F32) - assembled).astype(BF16)
                r_lhs[q, plane * 128:(plane + 1) * 128, lanes] = right
                if plane == 0:
                    r_neg[q, 128:256, lanes] = right
                else:
                    r_neg[q, 0:128, lanes] = -right
    v_sums = multiply(r_lhs, r_neg, g_buf, v_part, v_out, v_first, v_last, v_dout, v_dlast)
    for chunk in range(chunks5):
        v_sums.middle(chunk)
    v_hops = []
    for chunk in range(chunks5):
        v_cross[chunk] = v_sums.finish(chunk, 0).astype(BF16)
        v_hops.append(wire.send(v_cross.at[chunk], v_got.at[chunk], across))
    for chunk in range(chunks5):
        v_own[chunk] = v_sums.finish(chunk, 1)

    wire.recv(swap_got, y_swap)
    for at in range(per_q):
        lanes = slice(at * width2, (at + 1) * width2)
        for plane in range(2):
            mine = y_all[pl.ds(core * per_q + at, 1), plane, pl.ds(z, 1)].reshape(32, width2)
            theirs = y_swap[at, plane]
            for a in range(2):
                rows16 = slice(a * 16, a * 16 + 16)
                out1_ref[plane, pl.ds(pl.multiple_of((2 * a + core) * 16, 16), 16), lanes] = mine[rows16]
                out1_ref[plane, pl.ds(pl.multiple_of((2 * a + other) * 16, 16), 16), lanes] = theirs[rows16]
    width5 = v_part.shape[-1]
    for chunk in range(chunks5):
        wire.recv(v_hops[chunk], v_got.at[chunk])
        out2_ref[:, :, chunk * width5:(chunk + 1) * width5] = v_own[chunk] + v_got[chunk].astype(F32)
    wire.recycle()
    for group in range(groups):
        wire.sent_all(group, u_send.at[group, 0:15])
    wire.sent_all(groups, s4_out.at[0:15])


def local(child_rhs, child_inverse_t, boundary_tiles, boundary_lists, root_rhs, root_inverse):
    vmem = pltpu.VMEM
    pivots, own_q = child_inverse_t.shape[1], child_inverse_t.shape[2]
    bounds = boundary_tiles.shape[1]
    root_rows, root_cols = root_inverse.shape[1], root_inverse.shape[2]
    whole = pl.BlockSpec(memory_space=pltpu.VMEM)
    far = pl.BlockSpec(memory_space=pl.ANY)

    def scatter_scratch(width, chunks, split):
        w = width // chunks
        return [
            vmem((chunks, 2, 2, 4, 16, w), F32),
            vmem((split, 6, 2, 16, w), BF16),
            vmem((split, 2, 2, 16, w), BF16),
            vmem((split, 4, 2, 16, w), BF16),
            vmem((chunks - split, 3, 2, 2, 16, w), BF16),
            vmem((chunks - split, 3, 2, 2, 16, w), BF16),
        ]

    chunks2, chunks3, chunks5, groups = 4, 4, 3, 2
    w2 = 2 * own_q // chunks2
    blocks = bounds // groups // BLK
    w5 = root_rows // chunks5
    scratch = [
        vmem((2, 2, pivots, own_q), BF16),
        vmem((2, 2, bounds, own_q), BF16),
        vmem((2, 2, root_rows, root_cols), BF16),
        vmem((2, 8, 16, pivots), BF16),
        vmem((256, pivots), BF16),
        vmem((chunks2, 2, 4, 32, w2), F32),
        vmem((chunks2, 3, 2, 32, w2), BF16),
        vmem((chunks2, 3, 2, 32, w2), BF16),
        vmem((chunks2, 2, 4, 32, w2), BF16),
        vmem((2, 256, own_q), BF16),
        vmem((2, 256, own_q), BF16),
        vmem((chunks2 // 2, 2, 32, w2), BF16),
        *scatter_scratch(bounds, chunks3, SPLIT3),
        vmem((2, 16 * blocks, BLK), F32),
        vmem((groups, 16, 4 * blocks, BLK), BF16),
        vmem((groups, 2, 8, 4 * blocks, BLK), BF16),
        vmem((16, 2, 24, BLK), BF16),
        vmem((2, 2, 8, 4, 24, BLK), BF16),
        vmem((768, BLK), F32),
        vmem((groups, 384, 32 * blocks), BF16),
        vmem((2, 64), jnp.int32),
        vmem((2, root_cols, 256), BF16),
        vmem((2, 2, 128, root_cols), BF16),
        vmem((2, 128, root_cols), BF16),
        vmem((2, 256, root_cols), BF16),
        vmem((2, 256, root_cols), BF16),
        *scatter_scratch(root_rows, chunks5, SPLIT5),
        vmem((chunks5, 2, 16, w5), F32),
        vmem((chunks5, 2, 16, w5), BF16),
        vmem((chunks5, 2, 16, w5), BF16),
        pltpu.SemaphoreType.DMA((N_SENDS,)),
        pltpu.SemaphoreType.DMA((N_RECVS,)),
        pltpu.SemaphoreType.DMA((groups + 1,)),
        pltpu.SemaphoreType.DMA((groups + 1,)),
        pltpu.SemaphoreType.DMA((6,)),
        pltpu.SemaphoreType.REGULAR,
    ]
    shapes = (
        vmem((2, 64, own_q), BF16),
        vmem((2, 16, root_rows), F32),
    )
    child_t, root_t = pl.pallas_call(
        kernel,
        out_shape=shapes,
        in_specs=[far] * 6,
        out_specs=(whole, whole),
        scratch_shapes=scratch,
        compiler_params=pltpu.CompilerParams(
            collective_id=0, has_side_effects=True, vmem_limit_bytes=60 * 1024 * 1024
        ),
    )(
        jnp.transpose(child_rhs, (0, 2, 1)), child_inverse_t, boundary_tiles, boundary_lists, root_rhs, root_inverse
    )
    return jnp.transpose(child_t, (0, 2, 1)), jnp.transpose(root_t, (0, 2, 1))


def solution(mesh):
    return jax.shard_map(
        local,
        mesh=mesh,
        in_specs=(
            P(None, "row", "col"),
            P(None, "row", "col"),
            P(None, "row", "col"),
            P(),
            P(None, "col", None),
            P(None, "row", "col"),
        ),
        out_specs=(P(None, "col", "row"), P(None, "row", "col")),
        check_vma=False,
    )
```

```python
import jax
import jax.numpy as jnp
from jax import lax
from jax.experimental import pallas as pl
from jax.experimental.pallas import tpu as pltpu
from jax.sharding import PartitionSpec as P

MESH = pl.DeviceIdType.MESH
F32 = jnp.float32
BF16 = jnp.bfloat16
N_SENDS, N_RECVS = 39, 81
SPLIT3, SPLIT5 = 3, 1
CROSS, NEAR = 4, 2
BLK = 128
TILE = 256


class Wire:
    def __init__(self, send_sems, recv_sems, group_sends, group_recvs, here):
        self.send_sems, self.recv_sems, self.here = send_sems, recv_sems, here
        self.group_sends, self.group_recvs = group_sends, group_recvs
        self.count = self.high = 0
        self.free = []
        self.started = []

    def copy(self, src, dst, send_sem, recv_sem, device):
        return pltpu.make_async_remote_copy(
            src_ref=src, dst_ref=dst, send_sem=send_sem, recv_sem=recv_sem, device_id=device, device_id_type=MESH
        )

    def send(self, src, dst, device):
        at = self.count
        self.count += 1
        if self.free:
            slot = self.free.pop()
        else:
            slot = self.high
            self.high += 1
        copy = self.copy(src, dst, self.send_sems.at[slot], self.recv_sems.at[at], device)
        copy.start()
        self.started.append((slot, copy))
        return at

    def block(self, many):
        at, free = self.count, sorted(self.free)
        self.count += many
        for i in range(len(free) - many + 1):
            if free[i + many - 1] - free[i] == many - 1:
                self.free = free[:i] + free[i + many:]
                return at, free[i]
        slot = self.high
        self.high += many
        return at, slot

    def send_block(self, block, step, src, dst, device):
        self.copy(src, dst, self.send_sems.at[block[1] + step], self.recv_sems.at[block[0] + step], device).start()

    def sent_block(self, block, step, src, dst, device):
        at = block[1] + step
        self.started.append(
            (at, self.copy(src, dst, self.send_sems.at[at], self.recv_sems.at[block[0] + step], device))
        )

    def recv(self, at, dst):
        self.copy(dst, dst, self.send_sems.at[0], self.recv_sems.at[at], self.here).wait_recv()

    def recycle(self, keep=0):
        done = self.started[:len(self.started) - keep]
        self.started = self.started[len(done):]
        for slot, copy in done:
            copy.wait_send()
            self.free.append(slot)

    def send_in(self, group, src, dst, device):
        self.copy(src, dst, self.group_sends.at[group], self.group_recvs.at[group], device).start()

    def keep_in(self, group, src, dst):
        pltpu.make_async_copy(src, dst, self.group_recvs.at[group]).start()

    def recv_all(self, group, dst):
        self.copy(dst, dst, self.group_sends.at[group], self.group_recvs.at[group], self.here).wait_recv()

    def sent_all(self, group, src):
        self.copy(src, src, self.group_sends.at[group], self.group_recvs.at[group], self.here).wait_send()


class Ring:
    def __init__(self, me, up_device, down_device, far_device):
        self.me = me
        self.up, self.down, self.far = lax.rem(me + 1, 4), lax.rem(me + 3, 4), lax.rem(me + 2, 4)
        self.up_device, self.down_device, self.far_device = up_device, down_device, far_device


class Gather:
    def __init__(self, wire, ring, piece, source=None):
        self.wire, self.ring, self.piece = wire, ring, piece
        self.source = source or (lambda half: piece(half, ring.me))

    def start_half(self, half):
        w, r, piece = self.wire, self.ring, self.piece
        src = self.source(half)
        ahead, behind = (r.up_device, r.down_device) if half == 0 else (r.down_device, r.up_device)
        a = w.send(src, piece(half, r.me), ahead)
        b = w.send(src, piece(half, r.me), behind)
        if half == 0:
            self.a0, self.b0 = a, b
        else:
            self.a1, self.b1 = a, b

    def start(self):
        self.start_half(0)
        self.start_half(1)

    def forward(self):
        w, r, piece = self.wire, self.ring, self.piece
        w.recv(self.a0, piece(0, r.down))
        self.f0 = w.send(piece(0, r.down), piece(0, r.down), r.up_device)
        w.recv(self.a1, piece(1, r.up))
        self.f1 = w.send(piece(1, r.up), piece(1, r.up), r.down_device)

    def finish(self):
        w, r, piece = self.wire, self.ring, self.piece
        w.recv(self.b0, piece(0, r.up))
        w.recv(self.b1, piece(1, r.down))
        w.recv(self.f0, piece(0, r.far))
        w.recv(self.f1, piece(1, r.far))


class Reduce:
    def __init__(self, wire, ring, chunks, part, out, first, last):
        self.wire, self.ring, self.chunks, self.part = wire, ring, chunks, part
        self.out, self.first, self.last = out, first, last
        self.blocks = [wire.block(chunks) for _ in range(4)]
        self.late = {}

    def early(self, chunk):
        r, out, first, last = self.ring, self.out, self.first, self.last
        return (
            (0, r.far, out.at[chunk, 0], first.at[chunk, 0], r.up_device),
            (1, r.far, out.at[chunk, 1], first.at[chunk, 1], r.down_device),
            (1, r.up, out.at[chunk, 2], last.at[chunk, 0], r.up_device),
            (0, r.down, out.at[chunk, 3], last.at[chunk, 1], r.down_device),
        )

    def start(self, chunk):
        for block, (half, place, src, dst, device) in zip(self.blocks, self.early(chunk)):
            src[...] = self.part(chunk, half, place).astype(BF16)
            self.wire.send_block(block, chunk, src, dst, device)

    def started(self):
        for chunk in range(self.chunks):
            for block, (_, _, src, dst, device) in zip(self.blocks, self.early(chunk)):
                self.wire.sent_block(block, chunk, src, dst, device)

    def middle(self, chunk):
        w, r, out, first, last = self.wire, self.ring, self.out, self.first, self.last
        late = []
        for half, place, device in ((0, r.up, r.up_device), (1, r.down, r.down_device)):
            w.recv(self.blocks[half][0] + chunk, first.at[chunk, half])
            out[chunk, 4 + half] = (self.part(chunk, half, place) + first[chunk, half].astype(F32)).astype(BF16)
            late.append(w.send(out.at[chunk, 4 + half], last.at[chunk, 2 + half], device))
        self.late[chunk] = late

    def finish(self, chunk, half):
        w, last = self.wire, self.last
        w.recv(self.blocks[3 - half][0] + chunk, last.at[chunk, 1 - half])
        w.recv(self.late[chunk][half], last.at[chunk, 2 + half])
        return self.part(chunk, half, self.ring.me) + last[chunk, 1 - half].astype(F32) + last[chunk, 2 + half].astype(F32)


class DirectGather:
    def __init__(self, wire, ring, whole, three):
        self.wire, self.ring, self.whole, self.three = wire, ring, whole, three

    def start(self):
        w, r, whole = self.wire, self.ring, self.whole
        self.block = w.block(1)
        for to in (r.far_device, r.up_device, r.down_device):
            w.send_block(self.block, 0, whole(r.me), whole(r.me), to)
        w.sent_block(self.block, 0, self.three(), self.three(), w.here)

    def finish(self):
        self.wire.recv(self.block[0], self.three())


class DirectReduce:
    def __init__(self, wire, ring, chunks, part, out, last):
        self.wire, self.ring, self.chunks, self.part = wire, ring, chunks, part
        self.out, self.last = out, last
        self.block = wire.block(chunks)

    def copies(self, chunk):
        r = self.ring
        for at, (place, device) in enumerate(((r.far, r.far_device), (r.up, r.up_device), (r.down, r.down_device))):
            yield at, place, self.out.at[chunk, at], self.last.at[chunk, at], device

    def start(self, chunk):
        for at, place, src, dst, device in self.copies(chunk):
            for half in range(2):
                src[half] = self.part(chunk, half, place).astype(BF16)
            self.wire.send_block(self.block, chunk, src, dst, device)

    def started(self):
        for chunk in range(self.chunks):
            self.wire.sent_block(self.block, chunk, self.out.at[chunk], self.last.at[chunk], self.wire.here)

    def middle(self, chunk):
        pass

    def finish(self, chunk, half):
        if half == 0:
            self.wire.recv(self.block[0] + chunk, self.last.at[chunk])
        value = self.part(chunk, half, self.ring.me)
        for at in range(3):
            value = value + self.last[chunk, at, half].astype(F32)
        return value


class Mixed:
    def __init__(self, relayed, direct, split):
        self.relayed, self.direct, self.split = relayed, direct, split

    def middle(self, chunk):
        if chunk < self.split:
            self.relayed.middle(chunk)

    def finish(self, chunk, half):
        if chunk < self.split:
            return self.relayed.finish(chunk, half)
        return self.direct.finish(chunk - self.split, half)


def nt_dot(left, right):
    return lax.dot_general(left, right, (((1,), (1,)), ((), ())), preferred_element_type=F32)


def nn_dot(left, right):
    return jnp.dot(left, right, preferred_element_type=F32)


def iota(shape, axis):
    return lax.broadcasted_iota(jnp.int32, shape, axis).astype(F32)


def split_by(value, size):
    quotient = jnp.floor((value + 0.5) * (1.0 / size))
    return quotient, value - quotient * size


def kernel(
    b_hbm, a_hbm, f_hbm, lists_hbm, rhs_hbm, g_hbm, out1_ref, out2_ref,
    a_buf, f_buf, g_buf, b_all, b_neg,
    y_part, y_out, y_last, y_all, y_lhs, y_neg, y_swap,
    u_part, u_out, u_first, u_last, u_dout, u_dlast, u_flat, u_send,
    s4_in, s4_out, rr, rr_flat, onehot, lists_ref, rhs_ref, rhs_t, rhs_send, r_lhs, r_neg,
    v_part, v_out, v_first, v_last, v_dout, v_dlast, v_own, v_cross, v_got,
    send_sems, recv_sems, group_sends, group_recvs, local_sems, token_sem,
):
    row, col = lax.axis_index("row"), lax.axis_index("col")
    x_lo, z = lax.div(row, 4), lax.rem(row, 4)
    slot, core = lax.div(col, 2), lax.rem(col, 2)
    x_hi, y = lax.div(slot, 4), lax.rem(slot, 4)
    x = x_hi * 2 + x_lo
    other = 1 - core

    def device(x, y, z, core):
        return (lax.rem(x, 2) * 4 + z, lax.div(x, 2) * 8 + y * 2 + core)

    def place_of(row, slot):
        return (row, slot * 2 + core)

    across = place_of(row, lax.rem(slot + 4, 8))
    side = place_of(lax.rem(row + 4, 8), slot)
    partner = (row, slot * 2 + other)
    y_ring = Ring(
        y, device(x, lax.rem(y + 1, 4), z, core), device(x, lax.rem(y + 3, 4), z, core),
        device(x, lax.rem(y + 2, 4), z, core),
    )
    z_ring = Ring(
        z, device(x, y, lax.rem(z + 1, 4), core), device(x, y, lax.rem(z + 3, 4), core),
        device(x, y, lax.rem(z + 2, 4), core),
    )

    barrier = pltpu.get_barrier_semaphore()
    greet = [
        y_ring.up_device, y_ring.down_device, across, partner,
        z_ring.up_device, z_ring.down_device, z_ring.far_device, side,
    ]
    for peer in greet:
        pl.semaphore_signal(barrier, inc=1, device_id=peer, device_id_type=MESH)

    pivots = b_hbm.shape[2]

    def lanes_of(chunk, chunks):
        return pl.ds(chunk * (pivots // chunks), pivots // chunks)

    fetch = []

    def get(src, dst):
        copy = pltpu.make_async_copy(src, dst, local_sems.at[len(fetch)])
        copy.start()
        fetch.append(copy)
        return copy

    own_b = get(b_hbm, b_all.at[:, slot])
    own_lists = get(lists_hbm, lists_ref)
    own_rhs = get(rhs_hbm, rhs_ref)
    pl.semaphore_wait(barrier, len(greet))
    own_b.wait()

    wire = Wire(send_sems, recv_sems, group_sends, group_recvs, (row, col))

    def b_piece(chunk, chunks, x_half):
        return lambda half, place: b_all.at[half, x_half * 4 + place, :, lanes_of(chunk, chunks)]

    near, away, crossed = [], [], []
    for chunk in range(CROSS):
        crossed.append(wire.send(
            b_all.at[:, slot, :, lanes_of(chunk, CROSS)], b_all.at[:, slot, :, lanes_of(chunk, CROSS)], across
        ))
        if chunk < CROSS - 1:
            away.append(Gather(wire, y_ring, b_piece(chunk, CROSS, 1 - x_hi)))
        else:
            away.append(DirectGather(
                wire, y_ring, lambda place, chunk=chunk: b_all.at[:, (1 - x_hi) * 4 + place, :, lanes_of(chunk, CROSS)],
                lambda chunk=chunk: b_all.at[:, pl.ds((1 - x_hi) * 4, 3), :, lanes_of(chunk, CROSS)],
            ))
    for chunk in range(NEAR):
        near.append(Gather(
            wire, y_ring, b_piece(chunk, NEAR, x_hi),
        ))
        near[chunk].start()
    own_a = get(a_hbm, a_buf.at[core])
    a_got = [wire.send(a_hbm.at[plane], a_buf.at[core, plane], partner) for plane in range(2)]

    own_lists.wait()
    own_rhs.wait()
    cols = onehot.shape[2]
    blocks = u_send.shape[2] // 4
    t_block, t_rest = split_by(iota((384, cols), 0), 48)
    t_q, t_rest = split_by(t_rest, 24)
    t_col, t_at = split_by(t_rest, 6)
    s_chip, s_rest = split_by(iota((384, cols), 1), 4 * blocks)
    s_col, _ = split_by(s_rest, blocks)
    e_chip, e_rest = split_by(iota((64, cols), 1), 4 * blocks)
    _, e_at = split_by(e_rest, blocks)
    _, e_z = split_by(e_chip, 4)
    list_values = lists_ref[...].astype(F32).astype(BF16)
    for chunk in range(onehot.shape[0]):
        spread = (e_z * 16 + (chunk * blocks) + e_at == iota((64, cols), 0)).astype(BF16)
        spread_lists = nn_dot(list_values, spread)
        source_list = jnp.where(iota((1, cols), 1) < cols // 2, spread_lists[0:1], spread_lists[1:2])
        onehot[chunk] = jnp.where(
            (t_col == s_col) & (source_list == t_block * 12 + t_q * 6 + t_at), 1.0, 0.0
        ).astype(BF16)

    pick_slot, pick_rest = split_by(iota((128, 256), 0), 16)
    for mine in (False, True):
        parity = (core if mine else other).astype(F32)
        pick = (pick_slot * 32 + parity * 16 + pick_rest == iota((128, 256), 1)).astype(BF16)
        for plane in range(2):
            turned = nt_dot(pick, rhs_ref[plane]).astype(BF16)
            if mine:
                rhs_t[pl.ds(core, 1), plane] = turned[None]
            else:
                rhs_send[plane] = turned

    near[0].forward()
    for chunk in range(CROSS):
        wire.recv(crossed[chunk], b_all.at[:, (1 - x_hi) * 4 + y, :, lanes_of(chunk, CROSS)])
        away[chunk].start()
        if chunk + 1 < NEAR:
            near[chunk + 1].forward()
    for chunk in range(CROSS - 1):
        away[chunk].forward()
    own_a.wait()
    own_f = get(f_hbm, f_buf.at[core])
    for plane in range(2):
        wire.recv(a_got[plane], a_buf.at[other, plane])
    f_got = wire.send(f_hbm, f_buf.at[core], partner)
    rhs_got = wire.send(rhs_send, rhs_t.at[core], partner)
    for gather in near + away:
        gather.finish()
    wire.recycle(keep=2)

    b_neg[0:128] = -b_all[1].reshape(128, pivots)
    b_neg[128:256] = b_all[0].reshape(128, pivots)
    chunks2, width2 = y_part.shape[0], y_part.shape[-1]
    per_q = chunks2 // 2
    y_sums = DirectReduce(wire, z_ring, chunks2, lambda chunk, half, place: y_part[chunk, half, place], y_out, y_last)
    y_gathers = [
        DirectGather(
            wire, z_ring, lambda place, chunk=chunk: y_all.at[chunk, :, place],
            lambda chunk=chunk: y_all.at[chunk, :, pl.ds(0, 3)],
        )
        for chunk in range(chunks2)
    ]

    def s1_step(chunk, carry):
        q = lax.div(chunk, per_q)
        lanes = pl.ds(pl.multiple_of(lax.rem(chunk, per_q) * width2, width2), width2)
        value = nn_dot(b_all[...].reshape(256, pivots), a_buf[q, 0, :, lanes])
        value += nn_dot(b_neg[...], a_buf[q, 1, :, lanes])
        y_part[pl.ds(chunk, 1)] = value.reshape(1, 2, 4, 32, width2)
        y_sums.start(chunk)
        return carry

    lax.fori_loop(0, chunks2, s1_step, 0)
    y_sums.started()

    for chunk in range(chunks2):
        for half in range(2):
            y_all[chunk, half, pl.ds(z, 1)] = y_sums.finish(chunk, half).astype(BF16)[None]
        y_gathers[chunk].start()
    own_f.wait()
    own_g = get(g_hbm, g_buf.at[core])
    wire.recv(f_got, f_buf.at[other])
    wire.recycle(keep=chunks2)
    g_got = wire.send(g_hbm, g_buf.at[core], partner)
    for chunk in range(chunks2):
        y_gathers[chunk].finish()
        q, lanes = chunk // per_q, slice(chunk % per_q * width2, (chunk % per_q + 1) * width2)
        real, imag = y_all[chunk, 0].reshape(128, width2), y_all[chunk, 1].reshape(128, width2)
        y_lhs[q, 0:128, lanes] = real
        y_lhs[q, 128:256, lanes] = imag
        y_neg[q, 0:128, lanes] = -imag
        y_neg[q, 128:256, lanes] = real
    swap_got = wire.send(y_all.at[pl.ds(other * per_q, per_q), :, z], y_swap, partner)

    def multiply(lhs, neg, weights, part, out, first, last, direct_out, direct_last):
        chunks, width, split = part.shape[0], part.shape[-1], out.shape[0]

        def term(chunk, half, place):
            return part[chunk, :, (x_hi if half == 1 else 1 - x_hi), place]

        relayed = Reduce(wire, y_ring, split, term, out, first, last)
        direct = DirectReduce(
            wire, y_ring, chunks - split, lambda chunk, half, place: term(chunk + split, half, place),
            direct_out, direct_last,
        )

        def product(chunk):
            def tile_step(at, carry):
                src = pl.ds(pl.multiple_of(chunk * width + at * TILE, TILE), TILE)
                value = None
                for q in range(2):
                    for left, plane in ((lhs, 0), (neg, 1)):
                        product = nt_dot(left[q], weights[q, plane, src, :])
                        value = product if value is None else value + product
                where = pl.ds(pl.multiple_of(at * TILE, TILE), TILE)
                part[pl.ds(chunk, 1), :, :, :, :, where] = value.reshape(1, 2, 2, 4, 16, TILE)
                return carry

            lax.fori_loop(0, width // TILE, tile_step, 0)

        def relayed_step(chunk, carry):
            product(chunk)
            relayed.start(chunk)
            return carry

        def direct_step(chunk, carry):
            product(chunk + split)
            direct.start(chunk)
            return carry

        lax.fori_loop(0, split, relayed_step, 0)
        lax.fori_loop(0, chunks - split, direct_step, 0)
        relayed.started()
        direct.started()
        return Mixed(relayed, direct, split)

    chunks3 = u_part.shape[0]
    u_sums = multiply(y_lhs, y_neg, f_buf, u_part, u_out, u_first, u_last, u_dout, u_dlast)
    pl.semaphore_signal(token_sem, inc=1, device_id=side, device_id_type=MESH)
    for chunk in range(chunks3):
        u_sums.middle(chunk)

    def s4_row(x_step, z_step):
        return lax.rem(x_lo + x_step, 2) * 4 + lax.rem(z + z_step, 4)

    far_first = (2, 1, 3, 0)
    groups = u_send.shape[0]
    per_group = chunks3 // groups
    width_blocks = blocks // per_group
    for group in range(groups):
        for half in range(2):
            for part in range(per_group):
                update = u_sums.finish(group * per_group + part, half)
                for plane in range(2):
                    for block in range(width_blocks):
                        u_flat[plane, pl.ds(part * width_blocks + block, 16, stride=blocks), :] = (
                            update[plane][:, block * BLK:(block + 1) * BLK]
                        )
            u_send[group, half * 8:half * 8 + 8] = u_flat[...].astype(BF16).reshape(8, 4 * blocks, BLK)
            if group == 0 and half == 0:
                pl.semaphore_wait(token_sem, 1)
            to_slot = slot if half == 1 else lax.rem(slot + 4, 8)
            for z_step in far_first:
                for x_step in ((1, 0) if half == 1 else (0, 1)):
                    if half == 1 and x_step == 0 and z_step == 0:
                        continue
                    to_row = s4_row(x_step, z_step)
                    wire.send_in(
                        group, u_send.at[group, half * 8 + to_row], s4_in.at[group, x_hi, row], place_of(to_row, to_slot)
                    )
        wire.keep_in(group, u_send.at[group, 8 + row], s4_in.at[group, x_hi, row])
    for group in range(groups):
        wire.recv_all(group, s4_in.at[group])
    total = None
    for group in range(groups):
        for half in range(2):
            term = nn_dot(onehot[group], s4_in[group, half].reshape(cols, BLK))
            total = term if total is None else total + term
    packed = total.astype(BF16).reshape(8, 2, 24, BLK)
    s4_out[0:8] = packed
    s4_out[8:16] = packed
    for y_step in far_first:
        for half_step, x_step in ((1, 0), (1, 1), (0, 1), (0, 0)):
            if half_step == 0 and x_step == 0 and y_step == 0:
                continue
            to = (x_hi if half_step == 0 else 1 - x_hi) * 4 + lax.rem(y + y_step, 4)
            wire.send_in(
                groups, s4_out.at[x_step * 8 + to], rr.at[:, x_lo, slot, z], place_of(s4_row(x_step, 0), to)
            )
    wire.keep_in(groups, s4_out.at[slot], rr.at[:, x_lo, slot, z])
    wire.recv_all(groups, rr.at[:, :, :, z])

    r_gathers = [
        DirectGather(
            wire, z_ring, lambda place, q=q: rr.at[q, :, :, place], lambda q=q: rr.at[q, :, :, pl.ds(0, 3)]
        )
        for q in range(2)
    ]
    for q in range(2):
        r_gathers[q].start()
    own_g.wait()

    chunks5 = v_part.shape[0]
    wire.recv(rhs_got, rhs_t.at[other])
    wire.recv(g_got, g_buf.at[other])
    for q in range(2):
        r_gathers[q].finish()
        for plane in range(2):
            rr_flat[...] = rr[q, plane].astype(F32).reshape(rr_flat.shape)
            for block in range(6):
                lanes = slice(block * BLK, (block + 1) * BLK)
                assembled = rr_flat[pl.ds(block, 128, stride=6), :]
                right = (rhs_t[q, plane, :, lanes].astype(F32) - assembled).astype(BF16)
                r_lhs[q, plane * 128:(plane + 1) * 128, lanes] = right
                if plane == 0:
                    r_neg[q, 128:256, lanes] = right
                else:
                    r_neg[q, 0:128, lanes] = -right
    v_sums = multiply(r_lhs, r_neg, g_buf, v_part, v_out, v_first, v_last, v_dout, v_dlast)
    for chunk in range(chunks5):
        v_sums.middle(chunk)
    v_hops = []
    for chunk in range(chunks5):
        v_cross[chunk] = v_sums.finish(chunk, 0).astype(BF16)
        v_hops.append(wire.send(v_cross.at[chunk], v_got.at[chunk], across))
    for chunk in range(chunks5):
        v_own[chunk] = v_sums.finish(chunk, 1)

    wire.recv(swap_got, y_swap)
    for at in range(per_q):
        lanes = slice(at * width2, (at + 1) * width2)
        for plane in range(2):
            mine = y_all[pl.ds(core * per_q + at, 1), plane, pl.ds(z, 1)].reshape(32, width2)
            theirs = y_swap[at, plane]
            for a in range(2):
                rows16 = slice(a * 16, a * 16 + 16)
                out1_ref[plane, pl.ds(pl.multiple_of((2 * a + core) * 16, 16), 16), lanes] = mine[rows16]
                out1_ref[plane, pl.ds(pl.multiple_of((2 * a + other) * 16, 16), 16), lanes] = theirs[rows16]
    width5 = v_part.shape[-1]
    for chunk in range(chunks5):
        wire.recv(v_hops[chunk], v_got.at[chunk])
        out2_ref[:, :, chunk * width5:(chunk + 1) * width5] = v_own[chunk] + v_got[chunk].astype(F32)
    wire.recycle()
    for group in range(groups):
        wire.sent_all(group, u_send.at[group, 0:15])
    wire.sent_all(groups, s4_out.at[0:15])


def local(child_rhs, child_inverse_t, boundary_tiles, boundary_lists, root_rhs, root_inverse):
    vmem = pltpu.VMEM
    pivots, own_q = child_inverse_t.shape[1], child_inverse_t.shape[2]
    bounds = boundary_tiles.shape[1]
    root_rows, root_cols = root_inverse.shape[1], root_inverse.shape[2]
    whole = pl.BlockSpec(memory_space=pltpu.VMEM)
    far = pl.BlockSpec(memory_space=pl.ANY)

    def scatter_scratch(width, chunks, split):
        w = width // chunks
        return [
            vmem((chunks, 2, 2, 4, 16, w), F32),
            vmem((split, 6, 2, 16, w), BF16),
            vmem((split, 2, 2, 16, w), BF16),
            vmem((split, 4, 2, 16, w), BF16),
            vmem((chunks - split, 3, 2, 2, 16, w), BF16),
            vmem((chunks - split, 3, 2, 2, 16, w), BF16),
        ]

    chunks2, chunks3, chunks5, groups = 4, 4, 3, 2
    w2 = 2 * own_q // chunks2
    blocks = bounds // groups // BLK
    w5 = root_rows // chunks5
    scratch = [
        vmem((2, 2, pivots, own_q), BF16),
        vmem((2, 2, bounds, own_q), BF16),
        vmem((2, 2, root_rows, root_cols), BF16),
        vmem((2, 8, 16, pivots), BF16),
        vmem((256, pivots), BF16),
        vmem((chunks2, 2, 4, 32, w2), F32),
        vmem((chunks2, 3, 2, 32, w2), BF16),
        vmem((chunks2, 3, 2, 32, w2), BF16),
        vmem((chunks2, 2, 4, 32, w2), BF16),
        vmem((2, 256, own_q), BF16),
        vmem((2, 256, own_q), BF16),
        vmem((chunks2 // 2, 2, 32, w2), BF16),
        *scatter_scratch(bounds, chunks3, SPLIT3),
        vmem((2, 16 * blocks, BLK), F32),
        vmem((groups, 16, 4 * blocks, BLK), BF16),
        vmem((groups, 2, 8, 4 * blocks, BLK), BF16),
        vmem((16, 2, 24, BLK), BF16),
        vmem((2, 2, 8, 4, 24, BLK), BF16),
        vmem((768, BLK), F32),
        vmem((groups, 384, 32 * blocks), BF16),
        vmem((2, 64), jnp.int32),
        vmem((2, root_cols, 256), BF16),
        vmem((2, 2, 128, root_cols), BF16),
        vmem((2, 128, root_cols), BF16),
        vmem((2, 256, root_cols), BF16),
        vmem((2, 256, root_cols), BF16),
        *scatter_scratch(root_rows, chunks5, SPLIT5),
        vmem((chunks5, 2, 16, w5), F32),
        vmem((chunks5, 2, 16, w5), BF16),
        vmem((chunks5, 2, 16, w5), BF16),
        pltpu.SemaphoreType.DMA((N_SENDS,)),
        pltpu.SemaphoreType.DMA((N_RECVS,)),
        pltpu.SemaphoreType.DMA((groups + 1,)),
        pltpu.SemaphoreType.DMA((groups + 1,)),
        pltpu.SemaphoreType.DMA((6,)),
        pltpu.SemaphoreType.REGULAR,
    ]
    shapes = (
        vmem((2, 64, own_q), BF16),
        vmem((2, 16, root_rows), F32),
    )
    child_t, root_t = pl.pallas_call(
        kernel,
        out_shape=shapes,
        in_specs=[far] * 6,
        out_specs=(whole, whole),
        scratch_shapes=scratch,
        compiler_params=pltpu.CompilerParams(
            collective_id=0, has_side_effects=True, vmem_limit_bytes=60 * 1024 * 1024
        ),
    )(
        jnp.transpose(child_rhs, (0, 2, 1)), child_inverse_t, boundary_tiles, boundary_lists, root_rhs, root_inverse
    )
    return jnp.transpose(child_t, (0, 2, 1)), jnp.transpose(root_t, (0, 2, 1))


def solution(mesh):
    return jax.shard_map(
        local,
        mesh=mesh,
        in_specs=(
            P(None, "row", "col"),
            P(None, "row", "col"),
            P(None, "row", "col"),
            P(),
            P(None, "col", None),
            P(None, "row", "col"),
        ),
        out_specs=(P(None, "col", "row"), P(None, "row", "col")),
        check_vma=False,
    )
```
